256 devices in a mesh: tile: 16 (over x, y), depth: 16 (over z, core).
Axes of the slice: x: 4, y: 4, z: 8, core: 2. Of those that a mesh axis runs over, the one named last changes fastest.
Arguments:
- volume: bfloat16 [16, 16, 128, 128, 128], P('tile', 'depth'), may hold values from -8 to 8
- shear: float32 [16, 16, 2], P('tile', 'depth'), may hold values from -0.5 to 0.5
- absorb: float32 [16, 16], P('tile', 'depth'), may hold values from 0.000390625 to 0.0078125
- color_slope: float32 [3], replicated, may hold values from -3 to 3
- color_bias: float32 [3], replicated, may hold values from -1.5 to 1.5
- frag_tile: int32 [16, 16, 16, 1], P('tile', 'depth'), may hold values from 0 to 15; in each aligned block of 16 rows (0 to 15, 16 to 31, ..., all dimensions but the last counted through in order) at most 4 rows name the same one
- slot_perm: int32 [16, 16, 16, 16], P('tile', 'depth'), may hold values from 0 to 15, each once within a row
- frag_rows: int32 [16, 16, 16], P('tile', 'depth'), may hold values from 1 to 64
- tile_view: int32 [16], replicated, may hold values from 0 to 1
- tile_owner: int32 [16], replicated, may hold values from 0 to 15, each once
Outputs:
- frame: bfloat16 [16, 4, 256, 256], P('tile')
The draws below stay inside these ranges and needn't reach their ends.
Inputs may be any that keep to these rules, and one draw needn't show every extreme that they name: `frag_tile`: each brick puts at most 4 fragments on one screen tile, and some brick puts exactly 4 there in every draw. `slot_perm`: each row is a permutation of the positions. `tile_owner`: A permutation of the tiles.
All inputs are finite; a program needn't handle non-finite values.
Results may differ from the reference program's by a relative error of at most 0.0035.
Values may be sent and summed in bfloat16 or wider, within the bound.
No kernel may reach another device: no remote copies, remote signals or barrier semaphores. Data moves between devices by JAX's collectives and lax.ppermute only.
A program may use at most 64 MiB of HBM per device.

```python
import math
import jax
import jax.numpy as jnp
import numpy as np
from jax import lax

BRICK = 128
SAMPLES = 128
RAYS = 256
FRAG = 64
TILE_SIDE = 256
CAP = 4
FRAGS = 16
POS = 16
TILES = 16
SLABS = 16


def shared_view(key):
    shear_key = jax.random.fold_in(key, 7101)
    return jax.random.uniform(shear_key, (TILES, SLABS, 2), jnp.float32, -0.5, 0.5)


def draw_shear(key, part):
    return shared_view(key)


def draw_volume(key, part):
    shear_now = shared_view(key)
    frequency = jax.random.uniform(jax.random.fold_in(key, 7102), (TILES, SLABS, 2), jnp.float32, 0.8 * math.pi, 0.92 * math.pi)
    offset_angle = jax.random.uniform(jax.random.fold_in(key, 7103), (TILES, SLABS, 2), jnp.float32, -math.pi, math.pi)
    cell_pos = jnp.arange(BRICK).astype(jnp.float32)
    centred = cell_pos - (BRICK - 1) / 2.0
    row_shift = shear_now[:, :, 0][:, :, None] * centred[None, None, :]
    col_shift = shear_now[:, :, 1][:, :, None] * centred[None, None, :]
    row_wave = jnp.cos(frequency[:, :, 0][:, :, None, None] * (cell_pos[None, None, None, :] - row_shift[:, :, :, None]) + offset_angle[:, :, 0][:, :, None, None])
    col_wave = jnp.cos(frequency[:, :, 1][:, :, None, None] * (cell_pos[None, None, None, :] - col_shift[:, :, :, None]) + offset_angle[:, :, 1][:, :, None, None])
    jitter_key = jax.random.fold_in(key, 7104)
    full_shape = (TILES, SLABS, BRICK, BRICK, BRICK)
    jitter = 2.0 * jax.random.normal(jitter_key, full_shape, jnp.float32)
    volume = jitter + 3.0 * row_wave[:, :, :, :, None] + 3.0 * col_wave[:, :, :, None, :]
    return jnp.clip(volume, -8.0, 8.0).astype(jnp.bfloat16)


def plant(result, stream_key, smallest, top_value):
    longest = result.shape.index(max(result.shape))
    spots = []
    for shift in (0, 1):
        where = [jax.random.randint(jax.random.fold_in(stream_key, axis), (), 0, length) for axis, length in enumerate(result.shape)]
        where[longest] = (where[longest] + shift) % result.shape[longest]
        spots.append(tuple(where))
    return result.at[spots[0]].set(smallest).at[spots[1]].set(top_value)


def level_of(rng, extent, shards, least, high):
    level, own = 1.0, jax.random.fold_in(rng, 6)
    for axis_at, blocks in shards:
        heights = jnp.exp(jax.random.uniform(jax.random.fold_in(own, axis_at), (blocks,), jnp.float32, least / len(shards), high / len(shards)))
        level = level * jnp.repeat(heights, extent[axis_at] // blocks).reshape([-1 if axis == axis_at else 1 for axis in range(len(extent))])
    return level


def deal_out(own_key, own, number, rows, count, top, reach, slope):
    order = jax.random.permutation(own_key, count)
    heavy_load, ordinary = portions_of(count, rows * top, reach, slope, True), portions_of(count, rows * top, reach, slope, False)
    places = jnp.arange(count)

    def named(lengths, turn):
        used = int((lengths > 0).sum())
        fixed = max(1, used // 4)
        moved = fixed + (places - fixed + turn * (used - fixed)) % max(1, count - fixed)
        return jnp.zeros((count,), jnp.int32).at[order[jnp.where(places < fixed, places, moved)]].set(jnp.asarray(lengths, jnp.int32))

    lengths = jnp.where(number % 4 == 0, named(heavy_load, number // 4), named(ordinary, number - number // 4 - 1))
    mixed = jax.random.permutation(jax.random.fold_in(own, 3), count)
    giver, receiver = mixed[0:count // 2 * 2:2], mixed[1:count // 2 * 2:2]
    slack = jnp.minimum(lengths[giver] - 1, reach - lengths[receiver]) // 2
    slack = jnp.where((giver == order[0]) | (receiver == order[0]) | (lengths[receiver] == 0), 0, jnp.maximum(slack, 0))
    moved = jax.random.randint(jax.random.fold_in(own, 4), (count // 2,), 0, 1 << 20) % (slack + 1)
    lengths = lengths.at[giver].add(-moved).at[receiver].add(moved)
    labels = jnp.searchsorted(jnp.cumsum(lengths), jnp.arange(rows * top), side="right").astype(jnp.int32)
    table = labels.reshape(top, rows).T
    table = table[jax.random.permutation(jax.random.fold_in(own, 1), rows)]
    turn = jax.random.randint(jax.random.fold_in(own, 2), (rows, 1), 0, top)
    return jnp.take_along_axis(table, (jnp.arange(top)[None, :] + turn) % top, axis=1)


def portions_of(amount, total, limit, lean, full):
    portions = [(1 << 20) // math.isqrt(standing ** lean) + 1 for standing in range(1, amount + 1)]
    largest = limit if full else min(limit, max(-(-total // amount), total * portions[0] // sum(portions)))
    least = 1 if total - largest >= amount - 1 else 0
    holding, surplus = [largest] + [least] * (amount - 1), total - largest - least * (amount - 1)
    while surplus > 0:
        movable = [i for i in range(1, amount) if holding[i] < largest] or [i for i in range(1, amount) if holding[i] < limit]
        whole, remaining = sum([portions[i] for i in movable]), surplus
        for i in movable:
            extra = min(limit - holding[i], max(1, remaining * portions[i] // whole), surplus)
            holding[i] = holding[i] + extra
            surplus = surplus - extra
    return np.array(holding)


def setup_inputs(seed: int = 0) -> dict:
    seeds = jax.random.split(jax.random.key(seed), 11)
    volume = draw_volume(jax.random.fold_in(seeds[10], 71), 0)
    shear = draw_shear(jax.random.fold_in(seeds[10], 71), 0)
    absorb = jnp.clip(jnp.exp(math.log(0.0078125) - 2.9957323 * jax.random.uniform(seeds[2], (TILES, SLABS), jnp.float32) ** level_of(seeds[2], (TILES, SLABS), ((0, 16), (1, 16)), -0.2, 0.2)), 0.000390625, 0.0078125)
    color_slope = jnp.clip(jax.random.uniform(seeds[3], (3,), jnp.float32, -3.0, 3.0), -3.0, 3.0)
    color_bias = jnp.clip(jax.random.uniform(seeds[4], (3,), jnp.float32, -1.5, 1.5), -1.5, 1.5)
    frag_tile_keys = jax.random.split(jax.random.fold_in(seeds[5], 1), TILES * SLABS * FRAGS // FRAGS)
    frag_tile_turns = jax.random.permutation(jax.random.fold_in(seeds[5], 3), TILES * SLABS * FRAGS // FRAGS)
    frag_tile = jax.vmap(lambda own, number: deal_out(jax.random.fold_in(seeds[5], 2), own, number, FRAGS, TILES, 1, CAP, 2))(frag_tile_keys, frag_tile_turns).reshape((TILES, SLABS, FRAGS, 1))
    slot_perm = jax.vmap(lambda own: jax.random.permutation(own, POS))(jax.random.split(seeds[6], TILES * SLABS * TILES)).reshape((TILES, SLABS, TILES, POS)).astype(jnp.int32)
    frag_rows = plant(jax.random.randint(seeds[7], (TILES, SLABS, FRAGS), 1, FRAG + 1), jax.random.fold_in(seeds[7], 1), 1, FRAG).astype(jnp.int32)
    tile_view = plant(jax.random.randint(seeds[8], (TILES,), 0, 2), jax.random.fold_in(seeds[8], 1), 0, 1).astype(jnp.int32)
    tile_owner = jax.random.permutation(seeds[9], TILES).astype(jnp.int32)
    return {"volume": volume, "shear": shear, "absorb": absorb, "color_slope": color_slope, "color_bias": color_bias, "frag_tile": frag_tile, "slot_perm": slot_perm, "frag_rows": frag_rows, "tile_view": tile_view, "tile_owner": tile_owner}


def spline(offset):
    size_abs = jnp.abs(offset)
    inner = 2.0 / 3.0 - size_abs * size_abs + 0.5 * size_abs * size_abs * size_abs
    remain = 2.0 - size_abs
    outer = remain * remain * remain / 6.0
    return jnp.where(size_abs < 1.0, inner, jnp.where(size_abs < 2.0, outer, 0.0))


def tables(shear_pair, sample_index, side, rays, samples):
    cells = jnp.arange(side).astype(jnp.float32)
    depth_pos = (sample_index.astype(jnp.float32) + 0.5) * side / samples - 0.5
    ray_pos = (jnp.arange(rays).astype(jnp.float32) + 0.5) * side / rays - 0.5
    centred = depth_pos - (side - 1) / 2.0
    depth_table = spline(depth_pos[:, None] - cells[None, :])
    row_pos = ray_pos[None, :] + shear_pair[0] * centred[:, None]
    col_pos = ray_pos[None, :] + shear_pair[1] * centred[:, None]
    row_table = spline(row_pos[:, :, None] - cells[None, None, :])
    col_table = spline(col_pos[:, :, None] - cells[None, None, :])
    return depth_table.astype(jnp.bfloat16), row_table.astype(jnp.bfloat16), col_table.astype(jnp.bfloat16)


def render(brick, shear_pair, rate, color_slope, color_bias):
    side = brick.shape[0]
    sample_index = jnp.arange(SAMPLES, dtype=jnp.int32)
    depth_table, row_table, col_table = tables(shear_pair, sample_index, side, RAYS, SAMPLES)
    resampled = jnp.dot(depth_table, brick.reshape(side, side * side), preferred_element_type=jnp.float32)
    resampled = resampled.astype(jnp.bfloat16).reshape(SAMPLES, side, side)
    half_way = jnp.einsum("sua,sab->sub", row_table.astype(jnp.float32), resampled.astype(jnp.float32), precision=lax.Precision.HIGHEST).astype(jnp.bfloat16)
    field = jnp.einsum("sub,svb->suv", half_way.astype(jnp.float32), col_table.astype(jnp.float32), precision=lax.Precision.HIGHEST)
    softness = jax.nn.softplus(field)
    before = jnp.cumsum(softness, 0) - softness
    weight = jnp.exp(-rate * before) * (1.0 - jnp.exp(-rate * softness))
    colors = [jnp.sum(weight * jax.nn.sigmoid(color_slope[k] * field + color_bias[k]), 0) for k in range(3)]
    alpha = 1.0 - jnp.exp(-rate * jnp.sum(softness, 0))
    return jnp.stack(colors + [alpha]).astype(jnp.bfloat16)


def reference(volume, shear, absorb, color_slope, color_bias, frag_tile, slot_perm, frag_rows, tile_view, tile_owner):
    tiles = volume.shape[0]
    slabs = volume.shape[1]
    side = volume.shape[2]
    bricks = volume.reshape(tiles * slabs, side, side, side)
    shears = shear.reshape(tiles * slabs, 2)
    rates = absorb.reshape(tiles * slabs)
    images = lax.map(lambda item: render(item[0], item[1], item[2], color_slope, color_bias), (bricks, shears, rates))
    per_side = RAYS // FRAG
    frags = images.reshape(tiles, slabs, 4, per_side, FRAG, per_side, FRAG)
    frags = frags.transpose(0, 1, 3, 5, 2, 4, 6).reshape(tiles, slabs, per_side * per_side, 4, FRAG, FRAG)
    keep = jnp.arange(FRAG)[None, None, None, :] < frag_rows[:, :, :, None]
    frags = frags.astype(jnp.float32) * keep[:, :, :, None, :, None].astype(jnp.float32)
    target = frag_tile[:, :, :, 0]
    onehot = (target[..., None] == jnp.arange(tiles)[None, None, None, :]).astype(jnp.int32)
    rank = jnp.sum((jnp.cumsum(onehot, 2) - onehot) * onehot, -1).astype(jnp.int32)
    by_tile = jnp.take_along_axis(slot_perm, target[..., None].astype(jnp.int32), axis=2)
    position = jnp.take_along_axis(by_tile, rank[..., None], axis=3)[..., 0].astype(jnp.int32)
    slab_index = jnp.broadcast_to(jnp.arange(slabs, dtype=jnp.int32)[None, :, None], target.shape)
    layer = jnp.zeros((slabs, tiles, POS, 4, FRAG, FRAG), jnp.float32)
    layer = layer.at[slab_index, target, position].add(frags)
    flipped = tile_view[None, :, None, None, None, None] == 1
    ordered = jnp.where(flipped, layer[::-1], layer)
    clear = 1.0 - ordered[:, :, :, 3]
    running = jnp.cumprod(clear, 0)
    infront = jnp.concatenate([jnp.ones_like(running[:1]), running[:-1]], 0)
    color = jnp.sum(infront[:, :, :, None] * ordered[:, :, :, :3], 0)
    alpha = 1.0 - running[-1]
    composite = jnp.concatenate([color, alpha[:, :, None]], 2)
    per_tile = TILE_SIDE // FRAG
    composite = composite.reshape(tiles, per_tile, per_tile, 4, FRAG, FRAG).transpose(0, 3, 1, 4, 2, 5)
    composite = composite.reshape(tiles, 4, TILE_SIDE, TILE_SIDE).astype(jnp.bfloat16)
    return jnp.zeros_like(composite).at[tile_owner].set(composite)
```

```python
import math
import jax
import jax.numpy as jnp
import numpy as np
from jax import lax
from jax.experimental import pallas as pl
from jax.experimental.pallas import tpu as pltpu
from jax.sharding import PartitionSpec as P

SAMPLES = 128
RAYS = 256
SIDE = 128
STEP = 8
ROWS = RAYS // STEP
LOG2E = math.log2(math.e)
FRAG = 64
TILE_SIDE = 256
CAP = 4
POS = 16


def in_order(blocks, dim):
    shape = list(blocks.shape[1:])
    shape[dim] *= blocks.shape[0]
    return jnp.moveaxis(blocks, 0, dim).reshape(shape)


def one_gather(arrays, axis, dims):
    vector = jnp.concatenate([a.reshape(-1) for a in arrays])
    lines, at, outs = (lax.all_gather(vector, axis), 0, [])
    for a, dim in zip(arrays, dims):
        blocks = lines[:, at : at + a.size].reshape(-1, *a.shape)
        outs.append(in_order(blocks, dim))
        at += a.size
    return tuple(outs)


def sent_to_all(value, axis):
    copies = jnp.broadcast_to(value, (lax.axis_size(axis), *value.shape))
    return lax.all_to_all(copies, axis, split_axis=0, concat_axis=0, tiled=True)


def collect(value, axis, dim):
    return in_order(sent_to_all(value, axis), dim)


def spline(offset):
    size_abs = jnp.abs(offset)
    inner = 2.0 / 3.0 - size_abs * size_abs + 0.5 * size_abs * size_abs * size_abs
    remain = 2.0 - size_abs
    outer = remain * remain * remain / 6.0
    return jnp.where(size_abs < 1.0, inner, jnp.where(size_abs < 2.0, outer, 0.0))


def wrapped(diff):
    return jnp.bitwise_and(diff + 64, 127) - 64


def band(base, mask_ref):
    parts = []
    for k in range(SIDE // 16):
        part = pltpu.roll(base, 16 * k, 1) if k else base
        if k not in (3, 4):
            part = part * mask_ref[pl.ds(16 * k, 16), :]
        parts.append(part)
    return jnp.concatenate(parts, 0)


def render_kernel(par_ref, prev_ref, vol_ref, next_ref, out_ref, field_ref, cum_ref, clear_ref, acc_ref, mask_ref):
    step = pl.program_id(0)
    steps = SAMPLES // STEP
    slot = lax.rem(step, 2)
    w0 = float(np.float32(2.0 / 3.0).astype(jnp.bfloat16))
    w1 = float(np.float32(1.0 / 6.0).astype(jnp.bfloat16))

    @pl.when(step == 0)
    def _():
        r = lax.broadcasted_iota(jnp.int32, (SIDE, SIDE), 0)
        c = lax.broadcasted_iota(jnp.int32, (SIDE, SIDE), 1)
        mask_ref[...] = jnp.where(jnp.abs(r - c) < 64, 1.0, 0.0).astype(jnp.bfloat16)
        cum_ref[...] = jnp.zeros_like(cum_ref)
        clear_ref[...] = jnp.ones_like(clear_ref)
        acc_ref[...] = jnp.zeros_like(acc_ref)

    def make_field(j):
        s = step * STEP + j
        centred = s.astype(jnp.float32) - (SIDE - 1) / 2.0
        lo = jnp.maximum(j - 1, 0)
        hi = jnp.minimum(j + 1, STEP - 1)
        before = jnp.where(j == 0, prev_ref[0], vol_ref[lo]).astype(jnp.float32)
        after = jnp.where(j == STEP - 1, next_ref[0], vol_ref[hi]).astype(jnp.float32)
        wb = jnp.where(s == 0, 0.0, w1)
        wa = jnp.where(s == SAMPLES - 1, 0.0, w1)
        cells = (w0 * vol_ref[j].astype(jnp.float32) + (wb * before + wa * after)).astype(jnp.bfloat16)
        i = lax.broadcasted_iota(jnp.int32, (16, SIDE), 0)
        a = lax.broadcasted_iota(jnp.int32, (16, SIDE), 1)
        d_row = wrapped(i - a).astype(jnp.float32)
        d_col = wrapped(a - i).astype(jnp.float32)
        shift_r = par_ref[0] * centred
        shift_c = par_ref[1] * centred
        rows = jnp.concatenate(
            [band(spline(d_row + (shift_r + q)).astype(jnp.bfloat16), mask_ref) for q in (-0.25, 0.25)], 0
        )
        cols = jnp.concatenate(
            [band(spline(d_col + (shift_c + q)).astype(jnp.bfloat16), mask_ref) for q in (-0.25, 0.25)], 1
        )
        half = jnp.dot(rows, cells, preferred_element_type=jnp.float32).astype(jnp.bfloat16)
        field_ref[slot, j] = jnp.dot(half, cols, preferred_element_type=jnp.float32)

    def integrate(r):
        neg_rate = par_ref[2]
        for sub in range(ROWS // 8):
            at = pl.ds(pl.multiple_of(r * ROWS + 8 * sub, 8), 8)
            cum = cum_ref[at, :]
            clear = clear_ref[at, :]
            acc = [acc_ref[k, at, :] for k in range(3)]
            for j in range(STEP):
                f = field_ref[1 - slot, j, at, :]
                cum = cum + jnp.log(1.0 + jnp.exp2(f * LOG2E))
                after = jnp.exp2(neg_rate * cum)
                w = clear - after
                clear = after
                for k in range(3):
                    acc[k] = acc[k] + w * jnp.tanh(f * par_ref[3 + k] + par_ref[6 + k])
            cum_ref[at, :] = cum
            clear_ref[at, :] = clear
            for k in range(3):
                acc_ref[k, at, :] = acc[k]

    @pl.when(step == 0)
    def _():
        @pl.loop(0, STEP)
        def _(r):
            make_field(r)

    @pl.when((step > 0) & (step < steps))
    def _():
        @pl.loop(0, STEP)
        def _(r):
            make_field(r)
            integrate(r)

    @pl.when(step == steps)
    def _():
        @pl.loop(0, STEP)
        def _(r):
            integrate(r)

        r = lax.broadcasted_iota(jnp.int32, (RAYS, RAYS), 0)
        c = lax.broadcasted_iota(jnp.int32, (RAYS, RAYS), 1)
        half = RAYS // 2
        left = (c == jnp.bitwise_and(r, 1) * half + jnp.right_shift(r, 1)).astype(jnp.float32).astype(jnp.bfloat16)
        right = (r == jnp.bitwise_and(c, 1) * half + jnp.right_shift(c, 1)).astype(jnp.float32).astype(jnp.bfloat16)
        alpha = 1.0 - clear_ref[...]
        for k in range(4):
            plane = alpha if k == 3 else 0.5 * (alpha + acc_ref[k])
            plane = jnp.dot(left, plane.astype(jnp.bfloat16), preferred_element_type=jnp.float32)
            plane = jnp.dot(plane.astype(jnp.bfloat16), right, preferred_element_type=jnp.float32)
            out_ref[k] = plane.astype(jnp.bfloat16)


def render(brick, shear_pair, rate, slope, bias):
    params = jnp.concatenate([shear_pair, -LOG2E * rate[None], 0.5 * slope, 0.5 * bias])
    steps = SAMPLES // STEP
    at = lambda i: jnp.minimum(i, steps - 1)
    return pl.pallas_call(
        render_kernel,
        grid=(steps + 1,),
        in_specs=[
            pl.BlockSpec(memory_space=pltpu.SMEM),
            pl.BlockSpec((1, SIDE, SIDE), lambda i: (jnp.maximum(at(i) * STEP - 1, 0), 0, 0)),
            pl.BlockSpec((STEP, SIDE, SIDE), lambda i: (at(i), 0, 0)),
            pl.BlockSpec((1, SIDE, SIDE), lambda i: (jnp.minimum(at(i) * STEP + STEP, SAMPLES - 1), 0, 0)),
        ],
        out_specs=pl.BlockSpec((4, RAYS, RAYS), lambda i: (0, 0, 0)),
        out_shape=jax.ShapeDtypeStruct((4, RAYS, RAYS), jnp.bfloat16),
        scratch_shapes=[
            pltpu.VMEM((2, STEP, RAYS, RAYS), jnp.float32),
            pltpu.VMEM((RAYS, RAYS), jnp.float32),
            pltpu.VMEM((RAYS, RAYS), jnp.float32),
            pltpu.VMEM((3, RAYS, RAYS), jnp.float32),
            pltpu.VMEM((SIDE, SIDE), jnp.bfloat16),
        ],
        compiler_params=pltpu.CompilerParams(dimension_semantics=("arbitrary",), vmem_limit_bytes=32 * 2**20),
        name="render",
    )(params, brick, brick, brick)


def local(
    volume,
    shear,
    absorb,
    color_slope,
    color_bias,
    frag_tile,
    slot_perm,
    frag_rows,
    tile_view,
    tile_owner,
):
    brick = volume[0, 0]
    image = render(brick, shear[0, 0], absorb[0, 0], color_slope, color_bias)
    per_side = RAYS // FRAG
    count = per_side * per_side
    frags = image.reshape(4, per_side, FRAG, per_side, FRAG).transpose(1, 3, 0, 2, 4)
    keep = (jnp.arange(FRAG)[None, :] < frag_rows[0, 0][:, None]).astype(jnp.bfloat16)
    frags = (frags.reshape(count, 4, FRAG, FRAG) * keep[:, None, :, None]).reshape(
        count, 4 * FRAG * FRAG
    )
    group_size = lax.axis_size("tile")
    column = lax.axis_index("tile")
    target = frag_tile[0, 0, :, 0]
    onehot = (target[:, None] == jnp.arange(group_size)[None, :]).astype(jnp.int32)
    rank = jnp.sum((jnp.cumsum(onehot, 0) - onehot) * onehot, 1)
    row_perm = jnp.sum(onehot[:, :, None] * slot_perm[0, 0][None], 1)
    position = jnp.sum(row_perm * (rank[:, None] == jnp.arange(POS)[None, :]).astype(jnp.int32), 1)
    receiver = jnp.sum(onehot * tile_owner[None, :], 1)
    to_peer = receiver[:, None] == jnp.arange(group_size)[None, :]
    select = to_peer[:, :, None] & (rank[:, None, None] == jnp.arange(CAP)[None, None, :])
    select = select.reshape(count, group_size * CAP).T.astype(jnp.bfloat16)
    outgoing = jnp.dot(select, frags, preferred_element_type=jnp.float32).astype(jnp.bfloat16)
    incoming = lax.all_to_all(
        outgoing.reshape(group_size, CAP, 4 * FRAG * FRAG),
        "tile",
        split_axis=0,
        concat_axis=0,
        tiled=True,
    )
    all_receiver, all_rank, all_position = one_gather((receiver, rank, position), "tile", (0, 0, 0))
    mine = (all_receiver == column).reshape(group_size, count)
    at_place = (
        all_position.reshape(group_size, count)[:, :, None] == jnp.arange(POS)[None, None, :]
    ) & mine[:, :, None]
    at_slot = all_rank.reshape(group_size, count)[:, :, None] == jnp.arange(CAP)[None, None, :]
    place = jnp.einsum("sfp,sfk->psk", at_place.astype(jnp.float32), at_slot.astype(jnp.float32))
    place = place.reshape(POS, group_size * CAP).astype(jnp.bfloat16)
    layer = jnp.dot(
        place,
        incoming.reshape(group_size * CAP, 4 * FRAG * FRAG),
        preferred_element_type=jnp.float32,
    )
    per_tile = TILE_SIDE // FRAG
    tile_image = (
        layer.reshape(per_tile, per_tile, 4, FRAG, FRAG)
        .transpose(2, 0, 3, 1, 4)
        .reshape(4, TILE_SIDE, TILE_SIDE)
    )
    my_view = jnp.sum(jnp.where(tile_owner == column, tile_view, 0))
    slab_count = lax.axis_size("depth")
    strip_rows = TILE_SIDE // slab_count
    stacked = tile_image.reshape(4, slab_count, strip_rows * TILE_SIDE)
    gathered = lax.all_to_all(stacked, "depth", split_axis=1, concat_axis=1, tiled=True)
    ordered = jnp.where(my_view == 1, gathered[:, ::-1], gathered)
    running = jnp.cumprod(1.0 - ordered[3], 0)
    infront = jnp.concatenate([jnp.ones_like(running[:1]), running[:-1]], 0)
    color = jnp.sum(infront[None] * ordered[:3], 1)
    strip = jnp.concatenate([color, 1.0 - running[-1:]], 0).reshape(4, strip_rows, TILE_SIDE)
    finished = collect(strip.astype(jnp.bfloat16), "depth", 1)
    return finished[None]


def solution(mesh):
    in_specs = (
        P("tile", "depth", None, None, None),
        P("tile", "depth", None),
        P("tile", "depth"),
        P(),
        P(),
        P("tile", "depth", None, None),
        P("tile", "depth", None, None),
        P("tile", "depth", None),
        P(),
        P(),
    )
    out_specs = P("tile", None, None, None)
    return jax.shard_map(local, mesh=mesh, in_specs=in_specs, out_specs=out_specs, check_vma=False)
```

```python
import math
import jax
import jax.numpy as jnp
import numpy as np
from jax import lax
from jax.experimental import pallas as pl
from jax.experimental.pallas import tpu as pltpu
from jax.sharding import PartitionSpec as P

SAMPLES = 128
RAYS = 256
SIDE = 128
STEP = 8
BLOCKS = SAMPLES // STEP
ROWS = RAYS // STEP
LOG2E = math.log2(math.e)
GROUP = 16
DEVICES = 256
VMEM_LIMIT = 48 * 2**20
F32 = jnp.float32
BF16 = jnp.bfloat16


def iota(shape, dim):
    return lax.broadcasted_iota(jnp.int32, shape, dim)


def bits(value, shift, mask):
    return jnp.bitwise_and(jnp.right_shift(value, shift), mask)


def ones_where(condition):
    return jnp.where(condition, 1.0, 0.0).astype(BF16)


def spline(offset):
    size_abs = jnp.abs(offset)
    inner = 2.0 / 3.0 - size_abs * size_abs + 0.5 * size_abs * size_abs * size_abs
    remain = 2.0 - size_abs
    outer = remain * remain * remain / 6.0
    return jnp.where(size_abs < 1.0, inner, jnp.where(size_abs < 2.0, outer, 0.0))


def wrapped(diff):
    return jnp.bitwise_and(diff + 64, 127) - 64


def band(base, mask_ref):
    base = jnp.concatenate([base, pltpu.roll(base, 8, 1)], 0).astype(BF16)
    parts = []
    for k in range(SIDE // 16):
        part = pltpu.roll(base, 16 * k, 1) if k else base
        if k not in (3, 4):
            part = part * mask_ref[pl.ds(16 * k, 16), :]
        parts.append(part)
    return jnp.concatenate(parts, 0)


def render_kernel(
    shear_ref, rate_ref, slope_ref, bias_ref, live_ref, vol_hbm, out_ref,
    vol_ref, wide_ref, even_ref, odd_ref, cum_ref, clear_ref, acc_ref, mask_ref, plane_ref, pick_ref, sems,
):
    w0 = float(np.float32(2.0 / 3.0).astype(BF16))
    w1 = float(np.float32(1.0 / 6.0).astype(BF16))

    def chunk(k):
        at = pl.ds(k * STEP, STEP)
        return pltpu.make_async_copy(vol_hbm.at[at], vol_ref.at[at], sems.at[k])

    for k in range(BLOCKS):
        chunk(k).start()
    r = iota((SIDE, SIDE), 0)
    c = iota((SIDE, SIDE), 1)
    mask_ref[...] = ones_where(jnp.abs(r - c) < 64)
    cum_ref[...] = jnp.zeros_like(cum_ref)
    clear_ref[...] = jnp.ones_like(clear_ref)
    acc_ref[...] = jnp.zeros_like(acc_ref)
    wide_ref[3] = jnp.zeros((SIDE, SIDE), F32)
    chunk(0).wait()
    wide_ref[0] = vol_ref[0].astype(F32)

    def make_field(field_ref, block, j):
        s = block * STEP + j
        centred = s.astype(F32) - (SIDE - 1) / 2.0
        before = wide_ref[jnp.bitwise_and(s + 3, 3)]
        here = wide_ref[jnp.bitwise_and(s, 3)]
        alive = jnp.where(s == SAMPLES - 1, 0.0, 1.0)
        after = vol_ref[jnp.minimum(s + 1, SAMPLES - 1)].astype(F32) * alive
        wide_ref[jnp.bitwise_and(s + 1, 3)] = after
        cells = (w0 * here + w1 * (before + after)).astype(BF16)
        i = iota((8, SIDE), 0)
        a = iota((8, SIDE), 1)
        d_row = wrapped(i - a).astype(F32)
        d_col = wrapped(a - i).astype(F32)
        shift_r = shear_ref[0] * centred
        shift_c = shear_ref[1] * centred
        rows = jnp.concatenate([band(spline(d_row + (shift_r + q)), mask_ref) for q in (-0.25, 0.25)], 0)
        cols = jnp.concatenate([band(spline(d_col + (shift_c + q)), mask_ref) for q in (-0.25, 0.25)], 1)
        half = jnp.dot(rows, cells, preferred_element_type=F32).astype(BF16)
        field_ref[j] = jnp.dot(half, cols, preferred_element_type=F32)

    def integrate(field_ref, r):
        neg_rate = -LOG2E * rate_ref[0]
        slopes = [0.5 * slope_ref[k] for k in range(3)]
        biases = [0.5 * bias_ref[k] for k in range(3)]
        for sub in range(ROWS // 8):
            at = pl.ds(pl.multiple_of(r * ROWS + 8 * sub, 8), 8)
            cum = cum_ref[at, :]
            clear = clear_ref[at, :]
            acc = [acc_ref[k, at, :] for k in range(3)]
            for j in range(STEP):
                f = field_ref[j, at, :]
                cum = cum + jnp.log(1.0 + jnp.exp2(f * LOG2E))
                after = jnp.exp2(neg_rate * cum)
                w = clear - after
                clear = after
                for k in range(3):
                    acc[k] = acc[k] + w * jnp.tanh(f * slopes[k] + biases[k])
            cum_ref[at, :] = cum
            clear_ref[at, :] = clear
            for k in range(3):
                acc_ref[k, at, :] = acc[k]

    def fused(made_ref, used_ref, block):
        @pl.when(block + 1 < BLOCKS)
        def _():
            chunk(jnp.minimum(block + 1, BLOCKS - 1)).wait()

        @pl.loop(0, STEP)
        def _(r):
            make_field(made_ref, block, r)
            integrate(used_ref, r)

    chunk(1).wait()

    @pl.loop(0, STEP)
    def _(r):
        make_field(even_ref, 0, r)

    @pl.loop(0, BLOCKS // 2 - 1)
    def _(t):
        fused(odd_ref, even_ref, 2 * t + 1)
        fused(even_ref, odd_ref, 2 * t + 2)

    fused(odd_ref, even_ref, BLOCKS - 1)

    @pl.loop(0, STEP)
    def _(r):
        integrate(odd_ref, r)

    col = iota((8, RAYS), 1)
    lane_fv = bits(col, 5, 3)
    alpha = 1.0 - clear_ref[...]
    for k in range(4):
        plane_ref[k] = (alpha if k == 3 else 0.5 * (alpha + acc_ref[k])).astype(BF16)
    for fu in range(4):
        limit = jnp.zeros((8, RAYS), jnp.int32)
        for fv in range(4):
            limit = jnp.where(lane_fv == fv, live_ref[4 * fu + fv], limit)
        limit = jnp.concatenate([limit] * 4, 0)
        for par in range(2):
            at = pl.ds(128 * par + 32 * fu, 32)
            keep = ones_where(2 * iota((32, RAYS), 0) + par < limit)
            for k in range(4):
                plane_ref[k, at, :] = plane_ref[k, at, :] * keep
    lane = iota((1, RAYS), 1)
    src = iota((RAYS, RAYS), 0)
    for k in range(4):
        v = 128 * bits(lane, 7, 1) + 64 * bits(lane, 4, 1) + 16 * bits(bits(lane, 5, 3) - k, 0, 3) + bits(lane, 0, 15)
        select = ones_where(src == bits(v, 0, 1) * 128 + bits(v, 1, 127))
        got = jnp.dot(plane_ref[k], select, preferred_element_type=F32).astype(BF16)
        for fvh in range(2):
            pick_ref[k, fvh] = got[:, 128 * fvh : 128 * fvh + 128]
    turn = ones_where(src == bits(lane, 0, 15) * 16 + bits(lane, 4, 1) * 8 + bits(lane, 5, 7))
    block = bits(iota((16, 128), 1), 5, 3)
    for qb in range(4):
        masks = [ones_where(block == (k + qb) % 4) for k in range(4)]
        for g in range(2):
            stack = []
            for fu in range(4):
                for fvh in range(2):
                    for par in range(2):
                        at = pl.ds(128 * par + 32 * fu + 16 * g, 16)
                        picked = [pick_ref[k, fvh, at, :] * masks[k] for k in range(4)]
                        stack.append((picked[0] + picked[1]) + (picked[2] + picked[3]))
            lines = jnp.dot(turn, jnp.concatenate(stack, 0), preferred_element_type=F32).astype(BF16)
            out_ref[pl.ds((qb * 64 + 32 * g) * 8, 256), :] = lines


def render(brick, shear_pair, rate, slope, bias, live):
    smem = pl.BlockSpec(memory_space=pltpu.SMEM)
    return pl.pallas_call(
        render_kernel,
        in_specs=[smem] * 5 + [pl.BlockSpec(memory_space=pl.ANY)],
        out_specs=pl.BlockSpec(memory_space=pltpu.VMEM),
        out_shape=jax.ShapeDtypeStruct((DEVICES * 8, 128), BF16),
        scratch_shapes=[
            pltpu.VMEM((SAMPLES, SIDE, SIDE), BF16),
            pltpu.VMEM((4, SIDE, SIDE), F32),
            pltpu.VMEM((STEP, RAYS, RAYS), F32),
            pltpu.VMEM((STEP, RAYS, RAYS), F32),
            pltpu.VMEM((RAYS, RAYS), F32),
            pltpu.VMEM((RAYS, RAYS), F32),
            pltpu.VMEM((3, RAYS, RAYS), F32),
            pltpu.VMEM((SIDE, SIDE), BF16),
            pltpu.VMEM((4, RAYS, RAYS), BF16),
            pltpu.VMEM((4, 2, RAYS, 128), BF16),
            pltpu.SemaphoreType.DMA((BLOCKS,)),
        ],
        compiler_params=pltpu.CompilerParams(vmem_limit_bytes=VMEM_LIMIT),
        cost_estimate=pl.CostEstimate(flops=4 * 10**9, transcendentals=50 * 10**6, bytes_accessed=5 * 10**6),
        name="render",
    )(shear_pair, rate, slope, bias, live, brick)


def route_kernel(me_ref, target_ref, owner_ref, perm_ref, out_ref):
    frag = iota((16, 16), 0)
    tile = iota((16, 16), 1)
    target = jnp.broadcast_to(target_ref[...], (16, 16))
    onehot = jnp.where(target == tile, 1.0, 0.0)
    earlier = jnp.where(tile < frag, 1.0, 0.0)
    ahead = jnp.dot(earlier, onehot, preferred_element_type=F32)
    rank = jnp.sum(ahead * onehot, 1, keepdims=True)
    spots = jnp.dot(onehot, perm_ref[...].astype(F32), preferred_element_type=F32)
    position = jnp.sum(jnp.where(tile.astype(F32) == rank, spots, 0.0), 1, keepdims=True).astype(jnp.int32)
    owners = jnp.zeros((16, 16), jnp.int32)
    for t in range(16):
        owners = jnp.where(tile == t, owner_ref[t], owners)
    owner = jnp.sum(jnp.where(target == tile, owners, 0).astype(F32), 1, keepdims=True).astype(jnp.int32)
    key = bits(position, 0, 1) * 128 + owner * 8 + bits(position, 1, 7)
    key = jnp.broadcast_to(key, (16, 128)).astype(F32)
    f = iota((16, 128), 0)
    here = iota((16, 128), 1) == me_ref[0] * 8 + bits(f, 1, 7)
    lines = [
        jnp.sum(jnp.where(here & (bits(f, 0, 1) == f2), key, 0.0), 0, keepdims=True) for f2 in range(2)
    ]
    line = jnp.concatenate(lines, 0).astype(BF16)
    out_ref[...] = jnp.broadcast_to(line[None], (DEVICES, 2, 128))


def route(me, target, owner, perm):
    smem = pl.BlockSpec(memory_space=pltpu.SMEM)
    vmem = pl.BlockSpec(memory_space=pltpu.VMEM)
    return pl.pallas_call(
        route_kernel,
        in_specs=[smem, vmem, smem, vmem],
        out_specs=vmem,
        out_shape=jax.ShapeDtypeStruct((DEVICES, 2, 128), BF16),
        cost_estimate=pl.CostEstimate(flops=10**4, transcendentals=0, bytes_accessed=10**5),
        name="route",
    )(me, target, owner, perm)


def composite_kernel(me_ref, owner_ref, view_ref, key_ref, data_ref, out_ref):
    src = iota((RAYS, 128), 0)
    row_owner = bits(iota((128, 128), 0), 3, 15)
    flip = jnp.zeros((128, 128), jnp.int32)
    for t in range(16):
        flip = jnp.where(row_owner == owner_ref[t], view_ref[t], flip)
    flipped = jnp.concatenate([flip, flip], 0) == 1
    last = bits(3 + jnp.right_shift(me_ref[0], 2), 0, 3)
    lane = iota((1, RAYS), 1)
    channel = jnp.where(bits(lane, 4, 1) == 1, last, bits(lane, 5, 3))
    split = ones_where(iota((128, RAYS), 0) == channel * 32 + bits(lane, 7, 1) * 16 + bits(lane, 0, 15))
    row = iota((RAYS, 128), 0).astype(F32)

    def slab(d, carry):
        color, front = carry
        keys = jnp.sum(key_ref[:, d].astype(F32), 0)
        data = data_ref[:, d].reshape(128, 128)
        value = jnp.dot(data, split, preferred_element_type=F32).astype(BF16)
        value = jnp.concatenate([value[:, :128], value[:, 128:]], 0)
        place = jnp.concatenate([ones_where(row == keys[f2 : f2 + 1]) for f2 in range(2)], 1)
        layer = jnp.dot(place, value, preferred_element_type=F32)
        clear = 1.0 - pltpu.roll(layer, 112, 1)
        color = jnp.where(flipped, layer + clear * color, color + front * layer)
        return color, front * clear

    start = (jnp.zeros((RAYS, 128), F32), jnp.ones((RAYS, 128), F32))
    color, front = lax.fori_loop(0, GROUP, slab, start, unroll=4)
    lane = iota((RAYS, 128), 1)
    final = jnp.where(bits(lane, 5, 3) == last, 1.0 - front, color)
    low = bits(iota((128, 128), 1), 4, 1) == 0
    final = jnp.where(low, final[:128], pltpu.roll(final[128:], 16, 1)).astype(BF16)
    out_ref[...] = jnp.broadcast_to(final.reshape(GROUP, 1, 8, 128), (GROUP, GROUP, 8, 128))


def composite(me, owner, view, keys, data):
    smem = pl.BlockSpec(memory_space=pltpu.SMEM)
    vmem = pl.BlockSpec(memory_space=pltpu.VMEM)
    return pl.pallas_call(
        composite_kernel,
        in_specs=[smem, smem, smem, vmem, vmem],
        out_specs=vmem,
        out_shape=jax.ShapeDtypeStruct((GROUP, GROUP, 8, 128), BF16),
        compiler_params=pltpu.CompilerParams(vmem_limit_bytes=VMEM_LIMIT),
        cost_estimate=pl.CostEstimate(flops=10**9, transcendentals=0, bytes_accessed=10**6),
        name="composite",
    )(me, owner, view, keys.reshape(GROUP, GROUP, 2, 128), data.reshape(GROUP, GROUP, 8, 128))


def assemble_kernel(data_ref, out_ref, wide_ref, spot_ref):
    in_row = iota((1, 128), 1)
    turn = ones_where(iota((128, 128), 0) == bits(in_row, 0, 7) * 16 + bits(in_row, 3, 15))
    for qb in range(4):
        for g in range(4):
            lines = data_ref[pl.ds((qb * 64 + 16 * g) * 8, 128), :]
            lines = jnp.dot(turn, lines, preferred_element_type=F32).astype(BF16)
            for pp in range(8):
                at = pl.ds(64 * (pp // 2) + 16 * g, 16)
                wide_ref[at, pl.ds((qb * 2 + pp % 2) * 128, 128)] = lines[16 * pp : 16 * pp + 16]
    src = iota((128, RAYS), 0)
    v = iota((1, RAYS), 1)
    block = bits(src, 0, 31)
    for qb in range(4):
        for pch in range(2):
            hit = (bits(v, 7, 1) == pch) & (bits(v, 4, 3) == qb)
            at = jnp.where(hit, 16 * bits(v, 6, 1) + bits(v, 0, 15), 32)
            spot_ref[pl.ds((qb * 2 + pch) * 128, 128), :] = ones_where(block == at)
    wide_lane = iota((16, 8 * 128), 1)
    lane_ch = bits(bits(wide_lane, 5, 3) - bits(wide_lane, 8, 3), 0, 3)
    for k in range(4):
        mask = jnp.concatenate([ones_where(lane_ch == k)] * 16, 0)
        out_ref[0, k] = jnp.dot(wide_ref[...] * mask, spot_ref[...], preferred_element_type=F32).astype(BF16)


def assemble(data):
    return pl.pallas_call(
        assemble_kernel,
        in_specs=[pl.BlockSpec(memory_space=pltpu.VMEM)],
        out_specs=pl.BlockSpec(memory_space=pltpu.VMEM),
        out_shape=jax.ShapeDtypeStruct((1, 4, RAYS, RAYS), BF16),
        scratch_shapes=[pltpu.VMEM((RAYS, 1024), BF16), pltpu.VMEM((1024, RAYS), BF16)],
        compiler_params=pltpu.CompilerParams(vmem_limit_bytes=VMEM_LIMIT),
        cost_estimate=pl.CostEstimate(flops=10**9, transcendentals=0, bytes_accessed=10**6),
        name="assemble",
    )(data)


def exchange(blocks):
    return lax.all_to_all(blocks, ("tile", "depth"), split_axis=0, concat_axis=0, tiled=True)


def local(
    volume,
    shear,
    absorb,
    color_slope,
    color_bias,
    frag_tile,
    slot_perm,
    frag_rows,
    tile_view,
    tile_owner,
):
    me = lax.axis_index("tile").reshape(1)
    keys = exchange(route(me, frag_tile[0, 0], tile_owner, slot_perm[0, 0]))
    lines = render(volume[0, 0], shear[0, 0], absorb[0], color_slope, color_bias, frag_rows[0, 0])
    parts = exchange(lines.reshape(DEVICES, 8, 128))
    strips = composite(me, tile_owner, tile_view, keys, parts)
    finished = exchange(strips.reshape(DEVICES, 8, 128))
    return assemble(finished.reshape(DEVICES * 8, 128))


def solution(mesh):
    in_specs = (
        P("tile", "depth", None, None, None),
        P("tile", "depth", None),
        P("tile", "depth"),
        P(),
        P(),
        P("tile", "depth", None, None),
        P("tile", "depth", None, None),
        P("tile", "depth", None),
        P(),
        P(),
    )
    out_specs = P("tile", None, None, None)
    return jax.shard_map(local, mesh=mesh, in_specs=in_specs, out_specs=out_specs, check_vma=False)
```

```python
import math
import jax
import jax.numpy as jnp
import numpy as np
from jax import lax
from jax.experimental import pallas as pl
from jax.experimental.pallas import tpu as pltpu
from jax.sharding import PartitionSpec as P

SAMPLES = 128
RAYS = 256
SIDE = 128
STEP = 8
BLOCKS = SAMPLES // STEP
ROWS = RAYS // STEP
LOG2E = math.log2(math.e)
GROUP = 16
DEVICES = 256
LINES = 10
TOGETHER = 4
VMEM_LIMIT = 48 * 2**20
F32 = jnp.float32
BF16 = jnp.bfloat16


def iota(shape, dim):
    return lax.broadcasted_iota(jnp.int32, shape, dim)


def bits(value, shift, mask):
    return jnp.bitwise_and(jnp.right_shift(value, shift), mask)


def ones_where(condition):
    return jnp.where(condition, 1.0, 0.0).astype(BF16)


def spline(offset):
    size_abs = jnp.abs(offset)
    inner = 2.0 / 3.0 - size_abs * size_abs + 0.5 * size_abs * size_abs * size_abs
    remain = 2.0 - size_abs
    outer = remain * remain * remain / 6.0
    return jnp.where(size_abs < 1.0, inner, jnp.where(size_abs < 2.0, outer, 0.0))


def wrapped(diff):
    return jnp.bitwise_and(diff + 64, 127) - 64


def band(base, mask_ref):
    base = jnp.concatenate([base, pltpu.roll(base, 8, 1)], 0).astype(BF16)
    parts = []
    for k in range(SIDE // 16):
        part = pltpu.roll(base, 16 * k, 1) if k else base
        if k not in (3, 4):
            part = part * mask_ref[pl.ds(16 * k, 16), :]
        parts.append(part)
    return jnp.concatenate(parts, 0)


def key_lines(me, target_ref, owner_ref, perm):
    frag = iota((16, 16), 0)
    tile = iota((16, 16), 1)
    target = jnp.zeros((16, 16), jnp.int32)
    owners = jnp.zeros((16, 16), jnp.int32)
    for t in range(16):
        target = jnp.where(frag == t, target_ref[t], target)
        owners = jnp.where(tile == t, owner_ref[t], owners)
    onehot = jnp.where(target == tile, 1.0, 0.0)
    earlier = jnp.where(tile < frag, 1.0, 0.0)
    ahead = jnp.dot(earlier, onehot, preferred_element_type=F32)
    rank = jnp.sum(ahead * onehot, 1, keepdims=True)
    spots = jnp.dot(onehot, perm.astype(F32), preferred_element_type=F32)
    position = jnp.sum(jnp.where(tile.astype(F32) == rank, spots, 0.0), 1, keepdims=True).astype(jnp.int32)
    owner = jnp.sum(onehot * owners.astype(F32), 1, keepdims=True).astype(jnp.int32)
    key = bits(position, 0, 1) * 128 + owner * 8 + bits(position, 1, 7)
    key = jnp.broadcast_to(key, (16, 128)).astype(F32)
    f = iota((16, 128), 0)
    here = iota((16, 128), 1) == me * 8 + bits(f, 1, 7)
    return [jnp.sum(jnp.where(here & (bits(f, 0, 1) == f2), key, 0.0), 0, keepdims=True) for f2 in range(2)]


def render_kernel(
    me_ref, shear_hbm, rate_hbm, slope_hbm, bias_hbm, live_hbm, target_hbm, owner_hbm, perm_hbm, vol_hbm, out_ref,
    shear_ref, rate_ref, slope_ref, bias_ref, live_ref, target_ref, owner_ref, perm_ref,
    vol_ref, wide_ref, even_ref, odd_ref, cum_ref, clear_ref, acc_ref, mask_ref, plane_ref, pick_ref, fill_ref,
    sems, small_sems,
):
    small = (
        (shear_hbm, shear_ref), (rate_hbm, rate_ref), (slope_hbm, slope_ref), (bias_hbm, bias_ref),
        (live_hbm, live_ref), (target_hbm, target_ref), (owner_hbm, owner_ref), (perm_hbm, perm_ref),
    )
    small = [pltpu.make_async_copy(src, dst, small_sems.at[k]) for k, (src, dst) in enumerate(small)]
    for copy in small:
        copy.start()
    w0 = float(np.float32(2.0 / 3.0).astype(BF16))
    w1 = float(np.float32(1.0 / 6.0).astype(BF16))

    def chunk(k):
        at = pl.ds(k * STEP, STEP)
        return pltpu.make_async_copy(vol_hbm.at[at], vol_ref.at[at], sems.at[k])

    for k in range(BLOCKS):
        chunk(k).start()
    r = iota((SIDE, SIDE), 0)
    c = iota((SIDE, SIDE), 1)
    mask_ref[...] = ones_where(jnp.abs(r - c) < 64)
    cum_ref[...] = jnp.zeros_like(cum_ref)
    clear_ref[...] = jnp.ones_like(clear_ref)
    acc_ref[...] = jnp.zeros_like(acc_ref)
    wide_ref[3] = jnp.zeros((SIDE, SIDE), F32)
    for copy in small:
        copy.wait()
    key = key_lines(me_ref[0], target_ref, owner_ref, perm_ref[...])
    from_line = jnp.where(bits(iota((64, 128), 0), 0, 1) == 0, key[0], key[1]).astype(BF16)
    at = iota((1, 64), 1)
    spots = ones_where(iota((32 * LINES, 64), 0) == bits(at, 1, 31) * LINES + 8 + bits(at, 0, 1))
    fill_ref[...] = jnp.dot(spots, from_line, preferred_element_type=F32)
    chunk(0).wait()
    wide_ref[0] = vol_ref[0].astype(F32)

    def make_field(field_ref, block, j):
        s = block * STEP + j
        centred = s.astype(F32) - (SIDE - 1) / 2.0
        before = wide_ref[jnp.bitwise_and(s + 3, 3)]
        here = wide_ref[jnp.bitwise_and(s, 3)]
        alive = jnp.where(s >= SAMPLES - 1, 0.0, 1.0)
        after = vol_ref[jnp.minimum(s + 1, SAMPLES - 1)].astype(F32) * alive
        wide_ref[jnp.bitwise_and(s + 1, 3)] = after
        cells = (w0 * here + w1 * (before + after)).astype(BF16)
        i = iota((8, SIDE), 0)
        a = iota((8, SIDE), 1)
        d_row = wrapped(i - a).astype(F32)
        d_col = wrapped(a - i).astype(F32)
        shift_r = shear_ref[0] * centred
        shift_c = shear_ref[1] * centred
        rows = jnp.concatenate([band(spline(d_row + (shift_r + q)), mask_ref) for q in (-0.25, 0.25)], 0)
        cols = jnp.concatenate([band(spline(d_col + (shift_c + q)), mask_ref) for q in (-0.25, 0.25)], 1)
        half = jnp.dot(rows, cells, preferred_element_type=F32).astype(BF16)
        field_ref[j] = jnp.dot(half, cols, preferred_element_type=F32)

    def integrate(field_ref, r):
        neg_rate = -LOG2E * rate_ref[0, 0]
        slopes = [jnp.full((16, RAYS), 0.5 * slope_ref[k], F32).astype(BF16) for k in range(3)]
        biases = [jnp.full((16, RAYS), 0.5 * bias_ref[k], F32).astype(BF16) for k in range(3)]
        for sub in range(ROWS // 16):
            at = pl.ds(pl.multiple_of(r * ROWS + 16 * sub, 16), 16)
            cum = cum_ref[at, :]
            clear = clear_ref[at, :]
            terms = [[], [], []]
            for j in range(STEP):
                f = field_ref[j, at, :]
                cum = cum + jnp.log(1.0 + jnp.exp2(f * LOG2E))
                after = jnp.exp2(neg_rate * cum)
                w = (clear - after).astype(BF16)
                clear = after
                f = f.astype(BF16)
                for k in range(3):
                    terms[k].append(w * jnp.tanh(f * slopes[k] + biases[k]))
                    size = 1
                    while (j + 1) % (2 * size) == 0:
                        last = terms[k].pop()
                        terms[k][-1] = terms[k][-1] + last
                        size *= 2
            cum_ref[at, :] = cum
            clear_ref[at, :] = clear
            for k in range(3):
                acc_ref[k, at, :] += terms[k][0].astype(F32)

    def every(body):
        @pl.loop(0, STEP // TOGETHER)
        def _(r):
            for i in range(TOGETHER):
                body(TOGETHER * r + i)

    def fused(made_ref, used_ref, block):
        @pl.when(block + 1 < BLOCKS)
        def _():
            chunk(jnp.minimum(block + 1, BLOCKS - 1)).wait()

        def both(r):
            integrate(used_ref, r)
            make_field(made_ref, block, r)

        every(both)

    chunk(1).wait()
    every(lambda r: make_field(even_ref, 0, r))

    @pl.loop(0, BLOCKS // 2)
    def _(t):
        fused(odd_ref, even_ref, 2 * t + 1)
        fused(even_ref, odd_ref, 2 * t + 2)

    col = iota((8, RAYS), 1)
    lane_fv = bits(col, 5, 3)
    alpha = 1.0 - clear_ref[...]
    for k in range(4):
        plane_ref[k] = (alpha if k == 3 else 0.5 * (alpha + acc_ref[k])).astype(BF16)
    for fu in range(4):
        limit = jnp.zeros((8, RAYS), jnp.int32)
        for fv in range(4):
            limit = jnp.where(lane_fv == fv, live_ref[4 * fu + fv], limit)
        limit = jnp.concatenate([limit] * 4, 0)
        for par in range(2):
            at = pl.ds(128 * par + 32 * fu, 32)
            keep = ones_where(2 * iota((32, RAYS), 0) + par < limit)
            for k in range(4):
                plane_ref[k, at, :] = plane_ref[k, at, :] * keep
    lane = iota((1, RAYS), 1)
    src = iota((RAYS, RAYS), 0)
    for k in range(4):
        v = 128 * bits(lane, 7, 1) + 64 * bits(lane, 4, 1) + 16 * bits(bits(lane, 5, 3) - k, 0, 3) + bits(lane, 0, 15)
        select = ones_where(src == bits(v, 0, 1) * 128 + bits(v, 1, 127))
        got = jnp.dot(plane_ref[k], select, preferred_element_type=F32).astype(BF16)
        for fvh in range(2):
            pick_ref[k, fvh] = got[:, 128 * fvh : 128 * fvh + 128]
    spot = (bits(lane, 0, 15) * 2 + bits(lane, 4, 1)) * LINES + bits(lane, 5, 7)
    turn = ones_where(iota((32 * LINES, RAYS), 0) == spot)
    block = bits(iota((16, 128), 1), 5, 3)
    for qb in range(4):
        masks = [ones_where(block == (k + qb) % 4) for k in range(4)]
        for g in range(2):
            stack = []
            for fu in range(4):
                for fvh in range(2):
                    for par in range(2):
                        at = pl.ds(128 * par + 32 * fu + 16 * g, 16)
                        picked = [pick_ref[k, fvh, at, :] * masks[k] for k in range(4)]
                        stack.append((picked[0] + picked[1]) + (picked[2] + picked[3]))
            lines = jnp.dot(turn, jnp.concatenate(stack, 0), preferred_element_type=F32) + fill_ref[...]
            out_ref[pl.ds((qb * 64 + 32 * g) * LINES, 32 * LINES), :] = lines.astype(BF16)


def render(me, shear_pair, rate, slope, bias, live, target, owner, perm, brick):
    smem = pl.BlockSpec(memory_space=pltpu.SMEM)
    hbm = pl.BlockSpec(memory_space=pltpu.MemorySpace.HBM)
    return pl.pallas_call(
        render_kernel,
        in_specs=[smem] + [hbm] * 9,
        out_specs=pl.BlockSpec(memory_space=pltpu.VMEM),
        out_shape=jax.ShapeDtypeStruct((DEVICES * LINES, 128), BF16),
        scratch_shapes=[
            pltpu.SMEM((2,), F32),
            pltpu.SMEM((1, 1), F32),
            pltpu.SMEM((3,), F32),
            pltpu.SMEM((3,), F32),
            pltpu.SMEM((16,), jnp.int32),
            pltpu.SMEM((16,), jnp.int32),
            pltpu.SMEM((16,), jnp.int32),
            pltpu.VMEM((16, 16), jnp.int32),
            pltpu.VMEM((SAMPLES, SIDE, SIDE), BF16),
            pltpu.VMEM((4, SIDE, SIDE), F32),
            pltpu.VMEM((STEP, RAYS, RAYS), F32),
            pltpu.VMEM((STEP, RAYS, RAYS), F32),
            pltpu.VMEM((RAYS, RAYS), F32),
            pltpu.VMEM((RAYS, RAYS), F32),
            pltpu.VMEM((3, RAYS, RAYS), F32),
            pltpu.VMEM((SIDE, SIDE), BF16),
            pltpu.VMEM((4, RAYS, RAYS), BF16),
            pltpu.VMEM((4, 2, RAYS, 128), BF16),
            pltpu.VMEM((32 * LINES, 128), F32),
            pltpu.SemaphoreType.DMA((BLOCKS,)),
            pltpu.SemaphoreType.DMA((8,)),
        ],
        cost_estimate=pl.CostEstimate(flops=4 * 10**9, transcendentals=50 * 10**6, bytes_accessed=5 * 10**6),
        name="render",
    )(me, shear_pair, rate, slope, bias, live, target, owner, perm, brick)


def composite_kernel(me_ref, owner_ref, view_ref, data_ref, out_ref, frag_ref, key_ref):
    at = iota((1, 16 * LINES), 1)
    from_slab = jnp.right_shift(at * 205, 11)
    line = at - LINES * from_slab
    spot = jnp.where(line < 8, from_slab * 8 + line, 128 + (line - 8) * 16 + from_slab)
    undo = ones_where(iota((16 * LINES, 16 * LINES), 0) == spot)
    keys = jnp.zeros((32, 128), F32)
    for i in range(GROUP):
        lines = data_ref[pl.ds(16 * LINES * i, 16 * LINES), :]
        lines = jnp.dot(undo, lines, preferred_element_type=F32)
        frag_ref[i] = lines[:128].reshape(GROUP, 8, 128)
        keys = keys + lines[128:]
    key_ref[...] = keys
    src = iota((RAYS, 128), 0)
    row_owner = bits(iota((128, 128), 0), 3, 15)
    flip = jnp.zeros((128, 128), jnp.int32)
    for t in range(16):
        flip = jnp.where(row_owner == owner_ref[t], view_ref[t], flip)
    flipped = jnp.concatenate([flip, flip], 0) == 1
    last = bits(3 + jnp.right_shift(me_ref[0], 2), 0, 3)
    lane = iota((1, RAYS), 1)
    channel = jnp.where(bits(lane, 4, 1) == 1, last, bits(lane, 5, 3))
    split = ones_where(iota((128, RAYS), 0) == channel * 32 + bits(lane, 7, 1) * 16 + bits(lane, 0, 15))
    row = iota((RAYS, 128), 0).astype(F32)

    def slab(d, carry):
        color, front = carry
        keys = [key_ref[pl.ds(16 * f2 + d, 1), :] for f2 in range(2)]
        data = frag_ref[:, d].reshape(128, 128).astype(BF16)
        value = jnp.dot(data, split, preferred_element_type=F32).astype(BF16)
        value = jnp.concatenate([value[:, :128], value[:, 128:]], 0)
        place = jnp.concatenate([ones_where(row == keys[f2]) for f2 in range(2)], 1)
        layer = jnp.dot(place, value, preferred_element_type=F32)
        clear = 1.0 - pltpu.roll(layer, 112, 1)
        color = jnp.where(flipped, layer + clear * color, color + front * layer)
        return color, front * clear

    start = (jnp.zeros((RAYS, 128), F32), jnp.ones((RAYS, 128), F32))
    color, front = lax.fori_loop(0, GROUP, slab, start, unroll=4)
    lane = iota((RAYS, 128), 1)
    final = jnp.where(bits(lane, 5, 3) == last, 1.0 - front, color)
    low = bits(iota((128, 128), 1), 4, 1) == 0
    final = jnp.where(low, final[:128], pltpu.roll(final[128:], 16, 1)).astype(BF16)
    out_ref[...] = jnp.broadcast_to(final.reshape(GROUP, 1, 8, 128), (GROUP, GROUP, 8, 128))


def composite(me, owner, view, data):
    smem = pl.BlockSpec(memory_space=pltpu.SMEM)
    vmem = pl.BlockSpec(memory_space=pltpu.VMEM)
    return pl.pallas_call(
        composite_kernel,
        in_specs=[smem, smem, smem, vmem],
        out_specs=vmem,
        out_shape=jax.ShapeDtypeStruct((GROUP, GROUP, 8, 128), BF16),
        scratch_shapes=[pltpu.VMEM((GROUP, GROUP, 8, 128), F32), pltpu.VMEM((32, 128), F32)],
        compiler_params=pltpu.CompilerParams(vmem_limit_bytes=VMEM_LIMIT),
        cost_estimate=pl.CostEstimate(flops=10**9, transcendentals=0, bytes_accessed=10**6),
        name="composite",
    )(me, owner, view, data)


def assemble_kernel(data_ref, out_ref, wide_ref, spot_ref):
    in_row = iota((1, 128), 1)
    turn = ones_where(iota((128, 128), 0) == bits(in_row, 0, 7) * 16 + bits(in_row, 3, 15))
    for qb in range(4):
        for g in range(4):
            lines = data_ref[pl.ds((qb * 64 + 16 * g) * 8, 128), :]
            lines = jnp.dot(turn, lines, preferred_element_type=F32).astype(BF16)
            for pp in range(8):
                at = pl.ds(64 * (pp // 2) + 16 * g, 16)
                wide_ref[at, pl.ds((qb * 2 + pp % 2) * 128, 128)] = lines[16 * pp : 16 * pp + 16]
    src = iota((128, RAYS), 0)
    v = iota((1, RAYS), 1)
    block = bits(src, 0, 31)
    for qb in range(4):
        for pch in range(2):
            hit = (bits(v, 7, 1) == pch) & (bits(v, 4, 3) == qb)
            at = jnp.where(hit, 16 * bits(v, 6, 1) + bits(v, 0, 15), 32)
            spot_ref[pl.ds((qb * 2 + pch) * 128, 128), :] = ones_where(block == at)
    wide_lane = iota((16, 8 * 128), 1)
    lane_ch = bits(bits(wide_lane, 5, 3) - bits(wide_lane, 8, 3), 0, 3)
    for k in range(4):
        mask = jnp.concatenate([ones_where(lane_ch == k)] * 16, 0)
        out_ref[0, k] = jnp.dot(wide_ref[...] * mask, spot_ref[...], preferred_element_type=F32).astype(BF16)


def assemble(data):
    return pl.pallas_call(
        assemble_kernel,
        in_specs=[pl.BlockSpec(memory_space=pltpu.VMEM)],
        out_specs=pl.BlockSpec(memory_space=pltpu.VMEM),
        out_shape=jax.ShapeDtypeStruct((1, 4, RAYS, RAYS), BF16),
        scratch_shapes=[pltpu.VMEM((RAYS, 1024), BF16), pltpu.VMEM((1024, RAYS), BF16)],
        compiler_params=pltpu.CompilerParams(vmem_limit_bytes=VMEM_LIMIT),
        cost_estimate=pl.CostEstimate(flops=10**9, transcendentals=0, bytes_accessed=10**6),
        name="assemble",
    )(data)


def exchange(blocks):
    return lax.all_to_all(blocks, ("tile", "depth"), split_axis=0, concat_axis=0, tiled=True)


def local(
    volume,
    shear,
    absorb,
    color_slope,
    color_bias,
    frag_tile,
    slot_perm,
    frag_rows,
    tile_view,
    tile_owner,
):
    me = lax.axis_index("tile").reshape(1)
    lines = render(
        me, shear[0, 0], absorb, color_slope, color_bias, frag_rows[0, 0],
        frag_tile.reshape(16), tile_owner, slot_perm[0, 0], volume[0, 0],
    )
    parts = exchange(lines.reshape(DEVICES, LINES // 2, 2, 128))
    strips = composite(me, tile_owner, tile_view, parts.reshape(DEVICES * LINES, 128))
    finished = exchange(strips.reshape(DEVICES, 8, 128))
    return assemble(finished.reshape(DEVICES * 8, 128))


def solution(mesh):
    in_specs = (
        P("tile", "depth", None, None, None),
        P("tile", "depth", None),
        P("tile", "depth"),
        P(),
        P(),
        P("tile", "depth", None, None),
        P("tile", "depth", None, None),
        P("tile", "depth", None),
        P(),
        P(),
    )
    out_specs = P("tile", None, None, None)
    return jax.shard_map(local, mesh=mesh, in_specs=in_specs, out_specs=out_specs, check_vma=False)
```

```python
import math
import jax
import jax.numpy as jnp
import numpy as np
from jax import lax
from jax.experimental import pallas as pl
from jax.experimental.pallas import tpu as pltpu
from jax.sharding import PartitionSpec as P

SAMPLES = 128
RAYS = 256
SIDE = 128
STEP = 8
BLOCKS = SAMPLES // STEP
ROWS = RAYS // STEP
LOG2E = math.log2(math.e)
GROUP = 16
DEVICES = 256
LINES = 10
TOGETHER = 4
VMEM_LIMIT = 48 * 2**20
F32 = jnp.float32
BF16 = jnp.bfloat16


def iota(shape, dim):
    return lax.broadcasted_iota(jnp.int32, shape, dim)


def bits(value, shift, mask):
    return jnp.bitwise_and(jnp.right_shift(value, shift), mask)


def ones_where(condition):
    return jnp.where(condition, 1.0, 0.0).astype(BF16)


def spline(offset):
    size_abs = jnp.abs(offset)
    inner = 2.0 / 3.0 - size_abs * size_abs + 0.5 * size_abs * size_abs * size_abs
    remain = 2.0 - size_abs
    outer = remain * remain * remain / 6.0
    return jnp.where(size_abs < 1.0, inner, jnp.where(size_abs < 2.0, outer, 0.0))


def wrapped(diff):
    return jnp.bitwise_and(diff + 64, 127) - 64


def band(base, mask_ref):
    base = jnp.concatenate([base, pltpu.roll(base, 8, 1)], 0).astype(BF16)
    parts = []
    for k in range(SIDE // 16):
        part = pltpu.roll(base, 16 * k, 1) if k else base
        if k not in (3, 4):
            part = part * mask_ref[pl.ds(16 * k, 16), :]
        parts.append(part)
    return jnp.concatenate(parts, 0)


def key_lines(me, target_ref, owner_ref, perm):
    frag = iota((16, 16), 0)
    tile = iota((16, 16), 1)
    target = jnp.zeros((16, 16), jnp.int32)
    owners = jnp.zeros((16, 16), jnp.int32)
    for t in range(16):
        target = jnp.where(frag == t, target_ref[t], target)
        owners = jnp.where(tile == t, owner_ref[t], owners)
    onehot = jnp.where(target == tile, 1.0, 0.0)
    earlier = jnp.where(tile < frag, 1.0, 0.0)
    ahead = jnp.dot(earlier, onehot, preferred_element_type=F32)
    rank = jnp.sum(ahead * onehot, 1, keepdims=True)
    spots = jnp.dot(onehot, perm.astype(F32), preferred_element_type=F32)
    position = jnp.sum(jnp.where(tile.astype(F32) == rank, spots, 0.0), 1, keepdims=True).astype(jnp.int32)
    owner = jnp.sum(onehot * owners.astype(F32), 1, keepdims=True).astype(jnp.int32)
    key = bits(position, 0, 1) * 128 + owner * 8 + bits(position, 1, 7)
    key = jnp.broadcast_to(key, (16, 128)).astype(F32)
    f = iota((16, 128), 0)
    here = iota((16, 128), 1) == me * 8 + bits(f, 1, 7)
    return [jnp.sum(jnp.where(here & (bits(f, 0, 1) == f2), key, 0.0), 0, keepdims=True) for f2 in range(2)]


def render_kernel(
    me_ref, shear_hbm, rate_hbm, slope_hbm, bias_hbm, live_hbm, target_hbm, owner_hbm, perm_hbm, vol_hbm, out_ref,
    shear_ref, rate_ref, slope_ref, bias_ref, live_ref, target_ref, owner_ref, perm_ref,
    vol_ref, wide_ref, even_ref, odd_ref, cum_ref, clear_ref, acc_ref, mask_ref, plane_ref, pick_ref, fill_ref,
    sems, small_sems,
):
    small = (
        (shear_hbm, shear_ref), (rate_hbm, rate_ref), (slope_hbm, slope_ref), (bias_hbm, bias_ref),
        (live_hbm, live_ref), (target_hbm, target_ref), (owner_hbm, owner_ref), (perm_hbm, perm_ref),
    )
    small = [pltpu.make_async_copy(src, dst, small_sems.at[k]) for k, (src, dst) in enumerate(small)]
    for copy in small:
        copy.start()
    w0 = LOG2E * float(np.float32(2.0 / 3.0).astype(BF16))
    w1 = LOG2E * float(np.float32(1.0 / 6.0).astype(BF16))

    def chunk(k):
        at = pl.ds(k * STEP, STEP)
        return pltpu.make_async_copy(vol_hbm.at[at], vol_ref.at[at], sems.at[k])

    for k in range(BLOCKS):
        chunk(k).start()
    r = iota((SIDE, SIDE), 0)
    c = iota((SIDE, SIDE), 1)
    mask_ref[...] = ones_where(jnp.abs(r - c) < 64)
    cum_ref[...] = jnp.zeros_like(cum_ref)
    clear_ref[...] = jnp.ones_like(clear_ref)
    acc_ref[...] = jnp.zeros_like(acc_ref)
    wide_ref[3] = jnp.zeros((SIDE, SIDE), F32)
    vol_ref[SAMPLES] = jnp.zeros((SIDE, SIDE), BF16)
    for copy in small:
        copy.wait()
    key = key_lines(me_ref[0], target_ref, owner_ref, perm_ref[...])
    from_line = jnp.where(bits(iota((64, 128), 0), 0, 1) == 0, key[0], key[1]).astype(BF16)
    at = iota((1, 64), 1)
    spots = ones_where(iota((32 * LINES, 64), 0) == bits(at, 1, 31) * LINES + 8 + bits(at, 0, 1))
    fill_ref[...] = jnp.dot(spots, from_line, preferred_element_type=F32)
    chunk(0).wait()
    wide_ref[0] = vol_ref[0].astype(F32)

    def make_field(field_ref, block, j):
        s = block * STEP + j
        centred = s.astype(F32) - (SIDE - 1) / 2.0
        before = wide_ref[jnp.bitwise_and(s + 3, 3)]
        here = wide_ref[jnp.bitwise_and(s, 3)]
        after = vol_ref[jnp.minimum(s + 1, SAMPLES)].astype(F32)
        wide_ref[jnp.bitwise_and(s + 1, 3)] = after
        cells = (w0 * here + w1 * (before + after)).astype(BF16)
        i = iota((8, SIDE), 0)
        a = iota((8, SIDE), 1)
        d_row = wrapped(i - a).astype(F32)
        d_col = wrapped(a - i).astype(F32)
        shift_r = shear_ref[0] * centred
        shift_c = shear_ref[1] * centred
        rows = jnp.concatenate([band(spline(d_row + (shift_r + q)), mask_ref) for q in (-0.25, 0.25)], 0)
        cols = jnp.concatenate([band(spline(d_col + (shift_c + q)), mask_ref) for q in (-0.25, 0.25)], 1)
        half = jnp.dot(rows, cells, preferred_element_type=F32).astype(BF16)
        field_ref[j] = jnp.dot(half, cols, preferred_element_type=F32)

    def integrate(field_ref, r):
        neg_rate = -rate_ref[0, 0]
        slopes = [jnp.full((16, 128), (0.5 / LOG2E) * slope_ref[k], F32).astype(BF16) for k in range(3)]
        biases = [jnp.full((16, 128), 0.5 * bias_ref[k], F32).astype(BF16) for k in range(3)]
        for part in range(2 * (ROWS // 16)):
            sub, side = part // 2, pl.ds(128 * (part % 2), 128)
            at = pl.ds(pl.multiple_of(r * ROWS + 16 * sub, 16), 16)
            cum = cum_ref[at, side]
            clear = clear_ref[at, side]
            terms = [[], [], []]
            for j in range(STEP):
                f = field_ref[j, at, side]
                cum = cum + lax.log2(1.0 + jnp.exp2(f))
                after = jnp.exp2(neg_rate * cum)
                w = (clear - after).astype(BF16)
                clear = after
                f = f.astype(BF16)
                for k in range(3):
                    term = w * jnp.tanh(f * slopes[k] + biases[k])
                    terms[k] = [terms[k][0] + term] if terms[k] else [term]
            cum_ref[at, side] = cum
            clear_ref[at, side] = clear
            for k in range(3):
                acc_ref[k, at, side] += terms[k][0].astype(F32)

    def every(body):
        @pl.loop(0, STEP // TOGETHER)
        def _(r):
            for i in range(TOGETHER):
                body(TOGETHER * r + i)

    def fused(made_ref, used_ref, block):
        @pl.when(block + 1 < BLOCKS)
        def _():
            chunk(jnp.minimum(block + 1, BLOCKS - 1)).wait()

        def both(r):
            integrate(used_ref, r)
            make_field(made_ref, block, r)

        every(both)

    chunk(1).wait()
    every(lambda r: make_field(even_ref, 0, r))

    @pl.loop(0, BLOCKS // 2)
    def _(t):
        fused(odd_ref, even_ref, 2 * t + 1)
        fused(even_ref, odd_ref, 2 * t + 2)

    col = iota((8, RAYS), 1)
    lane_fv = bits(col, 5, 3)
    alpha = 1.0 - clear_ref[...]
    for k in range(4):
        plane_ref[k] = (alpha if k == 3 else 0.5 * (alpha + acc_ref[k])).astype(BF16)
    for fu in range(4):
        limit = jnp.zeros((8, RAYS), jnp.int32)
        for fv in range(4):
            limit = jnp.where(lane_fv == fv, live_ref[4 * fu + fv], limit)
        limit = jnp.concatenate([limit] * 4, 0)
        for par in range(2):
            at = pl.ds(128 * par + 32 * fu, 32)
            keep = ones_where(2 * iota((32, RAYS), 0) + par < limit)
            for k in range(4):
                plane_ref[k, at, :] = plane_ref[k, at, :] * keep
    lane = iota((1, RAYS), 1)
    src = iota((RAYS, RAYS), 0)
    for k in range(4):
        v = 128 * bits(lane, 7, 1) + 64 * bits(lane, 4, 1) + 16 * bits(bits(lane, 5, 3) - k, 0, 3) + bits(lane, 0, 15)
        select = ones_where(src == bits(v, 0, 1) * 128 + bits(v, 1, 127))
        got = jnp.dot(plane_ref[k], select, preferred_element_type=F32).astype(BF16)
        for fvh in range(2):
            pick_ref[k, fvh] = got[:, 128 * fvh : 128 * fvh + 128]
    spot = (bits(lane, 0, 15) * 2 + bits(lane, 4, 1)) * LINES + bits(lane, 5, 7)
    turn = ones_where(iota((32 * LINES, RAYS), 0) == spot)
    block = bits(iota((16, 128), 1), 5, 3)
    for qb in range(4):
        masks = [ones_where(block == (k + qb) % 4) for k in range(4)]
        for g in range(2):
            stack = []
            for fu in range(4):
                for fvh in range(2):
                    for par in range(2):
                        at = pl.ds(128 * par + 32 * fu + 16 * g, 16)
                        picked = [pick_ref[k, fvh, at, :] * masks[k] for k in range(4)]
                        stack.append((picked[0] + picked[1]) + (picked[2] + picked[3]))
            lines = jnp.dot(turn, jnp.concatenate(stack, 0), preferred_element_type=F32) + fill_ref[...]
            out_ref[pl.ds((qb * 64 + 32 * g) * LINES, 32 * LINES), :] = lines.astype(BF16)


def render(me, shear_pair, rate, slope, bias, live, target, owner, perm, brick):
    smem = pl.BlockSpec(memory_space=pltpu.SMEM)
    hbm = pl.BlockSpec(memory_space=pltpu.MemorySpace.HBM)
    return pl.pallas_call(
        render_kernel,
        in_specs=[smem] + [hbm] * 9,
        out_specs=pl.BlockSpec(memory_space=pltpu.VMEM),
        out_shape=jax.ShapeDtypeStruct((DEVICES * LINES, 128), BF16),
        scratch_shapes=[
            pltpu.SMEM((2,), F32),
            pltpu.SMEM((1, 1), F32),
            pltpu.SMEM((3,), F32),
            pltpu.SMEM((3,), F32),
            pltpu.SMEM((16,), jnp.int32),
            pltpu.SMEM((16,), jnp.int32),
            pltpu.SMEM((16,), jnp.int32),
            pltpu.VMEM((16, 16), jnp.int32),
            pltpu.VMEM((SAMPLES + 1, SIDE, SIDE), BF16),
            pltpu.VMEM((4, SIDE, SIDE), F32),
            pltpu.VMEM((STEP, RAYS, RAYS), F32),
            pltpu.VMEM((STEP, RAYS, RAYS), F32),
            pltpu.VMEM((RAYS, RAYS), F32),
            pltpu.VMEM((RAYS, RAYS), F32),
            pltpu.VMEM((3, RAYS, RAYS), F32),
            pltpu.VMEM((SIDE, SIDE), BF16),
            pltpu.VMEM((4, RAYS, RAYS), BF16),
            pltpu.VMEM((4, 2, RAYS, 128), BF16),
            pltpu.VMEM((32 * LINES, 128), F32),
            pltpu.SemaphoreType.DMA((BLOCKS,)),
            pltpu.SemaphoreType.DMA((8,)),
        ],
        cost_estimate=pl.CostEstimate(flops=4 * 10**9, transcendentals=50 * 10**6, bytes_accessed=5 * 10**6),
        name="render",
    )(me, shear_pair, rate, slope, bias, live, target, owner, perm, brick)


def composite_kernel(me_ref, owner_ref, view_ref, data_ref, out_ref, frag_ref, key_ref, layer_ref, flip_ref, color_ref, front_ref):
    at = iota((1, 16 * LINES), 1)
    from_slab = jnp.right_shift(at * 205, 11)
    line = at - LINES * from_slab
    spot = jnp.where(line < 8, from_slab * 8 + line, 128 + (line - 8) * 16 + from_slab)
    undo = ones_where(iota((16 * LINES, 16 * LINES), 0) == spot)
    keys = jnp.zeros((32, 128), F32)
    for i in range(GROUP):
        lines = data_ref[pl.ds(16 * LINES * i, 16 * LINES), :]
        lines = jnp.dot(undo, lines, preferred_element_type=F32)
        frag_ref[i] = lines[:128].reshape(GROUP, 8, 128)
        keys = keys + lines[128:]
    key_ref[...] = keys
    src = iota((RAYS, 128), 0)
    row_owner = bits(iota((128, 128), 0), 3, 15)
    flip = jnp.zeros((128, 128), jnp.int32)
    for t in range(16):
        flip = jnp.where(row_owner == owner_ref[t], view_ref[t], flip)
    flip_ref[...] = jnp.concatenate([flip, flip], 0)
    last = bits(3 + jnp.right_shift(me_ref[0], 2), 0, 3)
    lane = iota((1, RAYS), 1)
    channel = jnp.where(bits(lane, 4, 1) == 1, last, bits(lane, 5, 3))
    split = ones_where(iota((128, RAYS), 0) == channel * 32 + bits(lane, 7, 1) * 16 + bits(lane, 0, 15))
    row = iota((RAYS, 128), 0).astype(F32).astype(BF16)
    one, none = jnp.ones((RAYS, 128), BF16), jnp.zeros((RAYS, 128), BF16)

    @pl.loop(0, GROUP // 4)
    def _(t):
        for d in [4 * t + i for i in range(4)]:
            keys = [key_ref[pl.ds(16 * f2 + d, 1), :] for f2 in range(2)]
            data = frag_ref[:, d].reshape(128, 128).astype(BF16)
            value = jnp.dot(data, split, preferred_element_type=F32).astype(BF16)
            value = jnp.concatenate([value[:, :128], value[:, 128:]], 0)
            place = jnp.concatenate([jnp.where(row == keys[f2].astype(BF16), one, none) for f2 in range(2)], 1)
            layer_ref[d] = jnp.dot(place, value, preferred_element_type=F32)

    @pl.loop(0, RAYS // 64)
    def _(t):
        at = pl.ds(pl.multiple_of(64 * t, 64), 64)
        flipped = flip_ref[at, :] == 1
        color, front = jnp.zeros((64, 128), F32), jnp.ones((64, 128), F32)
        for d in range(GROUP):
            layer = layer_ref[d, at, :]
            clear = 1.0 - pltpu.roll(layer, 112, 1)
            color = jnp.where(flipped, layer + clear * color, color + front * layer)
            front = front * clear
        color_ref[at, :] = color
        front_ref[at, :] = front

    color, front = color_ref[...], front_ref[...]
    lane = iota((RAYS, 128), 1)
    final = jnp.where(bits(lane, 5, 3) == last, 1.0 - front, color)
    low = bits(iota((128, 128), 1), 4, 1) == 0
    final = jnp.where(low, final[:128], pltpu.roll(final[128:], 16, 1)).astype(BF16)
    out_ref[...] = jnp.broadcast_to(final.reshape(GROUP, 1, 8, 128), (GROUP, GROUP, 8, 128))


def composite(me, owner, view, data):
    smem = pl.BlockSpec(memory_space=pltpu.SMEM)
    vmem = pl.BlockSpec(memory_space=pltpu.VMEM)
    return pl.pallas_call(
        composite_kernel,
        in_specs=[smem, smem, smem, vmem],
        out_specs=vmem,
        out_shape=jax.ShapeDtypeStruct((GROUP, GROUP, 8, 128), BF16),
        scratch_shapes=[
            pltpu.VMEM((GROUP, GROUP, 8, 128), F32),
            pltpu.VMEM((32, 128), F32),
            pltpu.VMEM((GROUP, RAYS, 128), F32),
            pltpu.VMEM((RAYS, 128), jnp.int32),
            pltpu.VMEM((RAYS, 128), F32),
            pltpu.VMEM((RAYS, 128), F32),
        ],
        compiler_params=pltpu.CompilerParams(vmem_limit_bytes=VMEM_LIMIT),
        cost_estimate=pl.CostEstimate(flops=10**9, transcendentals=0, bytes_accessed=10**6),
        name="composite",
    )(me, owner, view, data)


def assemble_kernel(data_ref, out_ref, wide_ref, spot_ref):
    in_row = iota((1, 128), 1)
    turn = ones_where(iota((128, 128), 0) == bits(in_row, 0, 7) * 16 + bits(in_row, 3, 15))
    for qb in range(4):
        for g in range(4):
            lines = data_ref[pl.ds((qb * 64 + 16 * g) * 8, 128), :]
            lines = jnp.dot(turn, lines, preferred_element_type=F32).astype(BF16)
            for pp in range(8):
                at = pl.ds(64 * (pp // 2) + 16 * g, 16)
                wide_ref[at, pl.ds((qb * 2 + pp % 2) * 128, 128)] = lines[16 * pp : 16 * pp + 16]
    src = iota((128, RAYS), 0)
    v = iota((1, RAYS), 1)
    block = bits(src, 0, 31)
    for qb in range(4):
        for pch in range(2):
            hit = (bits(v, 7, 1) == pch) & (bits(v, 4, 3) == qb)
            at = jnp.where(hit, 16 * bits(v, 6, 1) + bits(v, 0, 15), 32)
            spot_ref[pl.ds((qb * 2 + pch) * 128, 128), :] = ones_where(block == at)
    wide_lane = iota((16, 8 * 128), 1)
    lane_ch = bits(bits(wide_lane, 5, 3) - bits(wide_lane, 8, 3), 0, 3)
    for k in range(4):
        mask = jnp.concatenate([ones_where(lane_ch == k)] * 16, 0)
        out_ref[0, k] = jnp.dot(wide_ref[...] * mask, spot_ref[...], preferred_element_type=F32).astype(BF16)


def assemble(data):
    return pl.pallas_call(
        assemble_kernel,
        in_specs=[pl.BlockSpec(memory_space=pltpu.VMEM)],
        out_specs=pl.BlockSpec(memory_space=pltpu.VMEM),
        out_shape=jax.ShapeDtypeStruct((1, 4, RAYS, RAYS), BF16),
        scratch_shapes=[pltpu.VMEM((RAYS, 1024), BF16), pltpu.VMEM((1024, RAYS), BF16)],
        compiler_params=pltpu.CompilerParams(vmem_limit_bytes=VMEM_LIMIT),
        cost_estimate=pl.CostEstimate(flops=10**9, transcendentals=0, bytes_accessed=10**6),
        name="assemble",
    )(data)


def exchange(blocks):
    return lax.all_to_all(blocks, ("tile", "depth"), split_axis=0, concat_axis=0, tiled=True)


def local(
    volume,
    shear,
    absorb,
    color_slope,
    color_bias,
    frag_tile,
    slot_perm,
    frag_rows,
    tile_view,
    tile_owner,
):
    me = lax.axis_index("tile").reshape(1)
    lines = render(
        me, shear[0, 0], absorb, color_slope, color_bias, frag_rows[0, 0],
        frag_tile.reshape(16), tile_owner, slot_perm[0, 0], volume[0, 0],
    )
    parts = exchange(lines.reshape(DEVICES, LINES // 2, 2, 128))
    strips = composite(me, tile_owner, tile_view, parts.reshape(DEVICES * LINES, 128))
    finished = exchange(strips.reshape(DEVICES, 8, 128))
    return assemble(finished.reshape(DEVICES * 8, 128))


def solution(mesh):
    in_specs = (
        P("tile", "depth", None, None, None),
        P("tile", "depth", None),
        P("tile", "depth"),
        P(),
        P(),
        P("tile", "depth", None, None),
        P("tile", "depth", None, None),
        P("tile", "depth", None),
        P(),
        P(),
    )
    out_specs = P("tile", None, None, None)
    return jax.shard_map(local, mesh=mesh, in_specs=in_specs, out_specs=out_specs, check_vma=False)
```

```python
import math
import jax
import jax.numpy as jnp
import numpy as np
from jax import lax
from jax.experimental import pallas as pl
from jax.experimental.pallas import tpu as pltpu
from jax.sharding import Mesh, PartitionSpec as P

SAMPLES = 128
RAYS = 256
SIDE = 128
STEP = 8
BLOCKS = SAMPLES // STEP
ROWS = RAYS // STEP
LOG2E = math.log2(math.e)
GROUP = 16
DEVICES = 256
CHIPS = 8
LINES = 10
TOGETHER = 4
VMEM_LIMIT = 48 * 2**20
F32 = jnp.float32
BF16 = jnp.bfloat16


def iota(shape, dim):
    return lax.broadcasted_iota(jnp.int32, shape, dim)


def bits(value, shift, mask):
    return jnp.bitwise_and(jnp.right_shift(value, shift), mask)


def ones_where(condition):
    return jnp.where(condition, 1.0, 0.0).astype(BF16)


def spline(offset):
    size_abs = jnp.abs(offset)
    inner = 2.0 / 3.0 - size_abs * size_abs + 0.5 * size_abs * size_abs * size_abs
    remain = 2.0 - size_abs
    outer = remain * remain * remain / 6.0
    return jnp.where(size_abs < 1.0, inner, jnp.where(size_abs < 2.0, outer, 0.0))


def wrapped(diff):
    return jnp.bitwise_and(diff + 64, 127) - 64


def band(base, mask_ref):
    base = jnp.concatenate([base, pltpu.roll(base, 8, 1)], 0).astype(BF16)
    parts = []
    for k in range(SIDE // 16):
        part = pltpu.roll(base, 16 * k, 1) if k else base
        if k not in (3, 4):
            part = part * mask_ref[pl.ds(16 * k, 16), :]
        parts.append(part)
    return jnp.concatenate(parts, 0)


def key_lines(me, target_ref, owner_ref, perm):
    frag = iota((16, 16), 0)
    tile = iota((16, 16), 1)
    target = jnp.zeros((16, 16), jnp.int32)
    owners = jnp.zeros((16, 16), jnp.int32)
    for t in range(16):
        target = jnp.where(frag == t, target_ref[t], target)
        owners = jnp.where(tile == t, owner_ref[t], owners)
    onehot = jnp.where(target == tile, 1.0, 0.0)
    earlier = jnp.where(tile < frag, 1.0, 0.0)
    ahead = jnp.dot(earlier, onehot, preferred_element_type=F32)
    rank = jnp.sum(ahead * onehot, 1, keepdims=True)
    spots = jnp.dot(onehot, perm.astype(F32), preferred_element_type=F32)
    position = jnp.sum(jnp.where(tile.astype(F32) == rank, spots, 0.0), 1, keepdims=True).astype(jnp.int32)
    owner = jnp.sum(onehot * owners.astype(F32), 1, keepdims=True).astype(jnp.int32)
    key = bits(position, 0, 1) * 128 + owner * 8 + bits(position, 1, 7)
    key = jnp.broadcast_to(key, (16, 128)).astype(F32)
    f = iota((16, 128), 0)
    here = iota((16, 128), 1) == me * 8 + bits(f, 1, 7)
    return [jnp.sum(jnp.where(here & (bits(f, 0, 1) == f2), key, 0.0), 0, keepdims=True) for f2 in range(2)]


def render_kernel(
    me_ref, shear_hbm, rate_hbm, slope_hbm, bias_hbm, live_hbm, target_hbm, owner_hbm, perm_hbm, vol_hbm, out_ref,
    shear_ref, rate_ref, slope_ref, bias_ref, live_ref, target_ref, owner_ref, perm_ref,
    vol_ref, wide_ref, even_ref, odd_ref, cum_ref, clear_ref, acc_ref, mask_ref, plane_ref, pick_ref, fill_ref,
    sems, small_sems,
):
    small = (
        (shear_hbm, shear_ref), (rate_hbm, rate_ref), (slope_hbm, slope_ref), (bias_hbm, bias_ref),
        (live_hbm, live_ref), (target_hbm, target_ref), (owner_hbm, owner_ref), (perm_hbm, perm_ref),
    )
    small = [pltpu.make_async_copy(src, dst, small_sems.at[k]) for k, (src, dst) in enumerate(small)]
    for copy in small:
        copy.start()
    w0 = LOG2E * float(np.float32(2.0 / 3.0).astype(BF16))
    w1 = LOG2E * float(np.float32(1.0 / 6.0).astype(BF16))

    def chunk(k):
        at = pl.ds(k * STEP, STEP)
        return pltpu.make_async_copy(vol_hbm.at[at], vol_ref.at[at], sems.at[k])

    for k in range(BLOCKS):
        chunk(k).start()
    r = iota((SIDE, SIDE), 0)
    c = iota((SIDE, SIDE), 1)
    mask_ref[...] = ones_where(jnp.abs(r - c) < 64)
    cum_ref[...] = jnp.zeros_like(cum_ref)
    clear_ref[...] = jnp.ones_like(clear_ref)
    acc_ref[...] = jnp.zeros_like(acc_ref)
    wide_ref[3] = jnp.zeros((SIDE, SIDE), F32)
    vol_ref[SAMPLES] = jnp.zeros((SIDE, SIDE), BF16)
    for copy in small:
        copy.wait()
    key = key_lines(me_ref[0], target_ref, owner_ref, perm_ref[...])
    from_line = jnp.where(bits(iota((64, 128), 0), 0, 1) == 0, key[0], key[1]).astype(BF16)
    at = iota((1, 64), 1)
    spots = ones_where(iota((32 * LINES, 64), 0) == bits(at, 1, 31) * LINES + 8 + bits(at, 0, 1))
    fill_ref[...] = jnp.dot(spots, from_line, preferred_element_type=F32)
    chunk(0).wait()
    wide_ref[0] = vol_ref[0].astype(F32)

    def make_field(field_ref, block, j):
        s = block * STEP + j
        centred = s.astype(F32) - (SIDE - 1) / 2.0
        before = wide_ref[jnp.bitwise_and(s + 3, 3)]
        here = wide_ref[jnp.bitwise_and(s, 3)]
        after = vol_ref[jnp.minimum(s + 1, SAMPLES)].astype(F32)
        wide_ref[jnp.bitwise_and(s + 1, 3)] = after
        cells = (w0 * here + w1 * (before + after)).astype(BF16)
        i = iota((8, SIDE), 0)
        a = iota((8, SIDE), 1)
        d_row = wrapped(i - a).astype(F32)
        d_col = wrapped(a - i).astype(F32)
        shift_r = shear_ref[0] * centred
        shift_c = shear_ref[1] * centred
        rows = jnp.concatenate([band(spline(d_row + (shift_r + q)), mask_ref) for q in (-0.25, 0.25)], 0)
        cols = jnp.concatenate([band(spline(d_col + (shift_c + q)), mask_ref) for q in (-0.25, 0.25)], 1)
        half = jnp.dot(rows, cells, preferred_element_type=F32).astype(BF16)
        field_ref[j] = jnp.dot(half, cols, preferred_element_type=F32)

    def integrate(field_ref, r):
        neg_rate = -rate_ref[0, 0]
        slopes = [jnp.full((16, 128), (0.5 / LOG2E) * slope_ref[k], F32).astype(BF16) for k in range(3)]
        biases = [jnp.full((16, 128), 0.5 * bias_ref[k], F32).astype(BF16) for k in range(3)]
        for part in range(2 * (ROWS // 16)):
            sub, side = part // 2, pl.ds(128 * (part % 2), 128)
            at = pl.ds(pl.multiple_of(r * ROWS + 16 * sub, 16), 16)
            cum = cum_ref[at, side]
            clear = clear_ref[at, side]
            terms = [[], [], []]
            for j in range(STEP):
                f = field_ref[j, at, side]
                cum = cum + lax.log2(1.0 + jnp.exp2(f))
                after = jnp.exp2(neg_rate * cum)
                w = (clear - after).astype(BF16)
                clear = after
                f = f.astype(BF16)
                for k in range(3):
                    terms[k].append(w * jnp.tanh(f * slopes[k] + biases[k]))
                    size = 1
                    while (j + 1) % (2 * size) == 0:
                        last = terms[k].pop()
                        terms[k][-1] = terms[k][-1] + last
                        size *= 2
            cum_ref[at, side] = cum
            clear_ref[at, side] = clear
            for k in range(3):
                acc_ref[k, at, side] += terms[k][0].astype(F32)

    def every(body):
        @pl.loop(0, STEP // TOGETHER)
        def _(r):
            for i in range(TOGETHER):
                body(TOGETHER * r + i)

    def fused(made_ref, used_ref, block):
        @pl.when(block + 1 < BLOCKS)
        def _():
            chunk(jnp.minimum(block + 1, BLOCKS - 1)).wait()

        def both(r):
            integrate(used_ref, r)
            make_field(made_ref, block, r)

        every(both)

    chunk(1).wait()
    every(lambda r: make_field(even_ref, 0, r))

    @pl.loop(0, BLOCKS // 2)
    def _(t):
        fused(odd_ref, even_ref, 2 * t + 1)
        fused(even_ref, odd_ref, 2 * t + 2)

    col = iota((8, RAYS), 1)
    lane_fv = bits(col, 5, 3)
    alpha = 1.0 - clear_ref[...]
    for k in range(4):
        plane_ref[k] = (alpha if k == 3 else 0.5 * (alpha + acc_ref[k])).astype(BF16)
    for fu in range(4):
        limit = jnp.zeros((8, RAYS), jnp.int32)
        for fv in range(4):
            limit = jnp.where(lane_fv == fv, live_ref[4 * fu + fv], limit)
        limit = jnp.concatenate([limit] * 4, 0)
        for par in range(2):
            at = pl.ds(128 * par + 32 * fu, 32)
            keep = ones_where(2 * iota((32, RAYS), 0) + par < limit)
            for k in range(4):
                plane_ref[k, at, :] = plane_ref[k, at, :] * keep
    lane = iota((1, RAYS), 1)
    src = iota((RAYS, RAYS), 0)
    for k in range(4):
        v = 128 * bits(lane, 7, 1) + 64 * bits(lane, 4, 1) + 16 * bits(bits(lane, 5, 3) - k, 0, 3) + bits(lane, 0, 15)
        select = ones_where(src == bits(v, 0, 1) * 128 + bits(v, 1, 127))
        got = jnp.dot(plane_ref[k], select, preferred_element_type=F32).astype(BF16)
        for fvh in range(2):
            pick_ref[k, fvh] = got[:, 128 * fvh : 128 * fvh + 128]
    spot = (bits(lane, 0, 15) * 2 + bits(lane, 4, 1)) * LINES + bits(lane, 5, 7)
    turn = ones_where(iota((32 * LINES, RAYS), 0) == spot)
    block = bits(iota((16, 128), 1), 5, 3)
    for qb in range(4):
        masks = [ones_where(block == (k + qb) % 4) for k in range(4)]
        for g in range(2):
            stack = []
            for fu in range(4):
                for fvh in range(2):
                    for par in range(2):
                        at = pl.ds(128 * par + 32 * fu + 16 * g, 16)
                        picked = [pick_ref[k, fvh, at, :] * masks[k] for k in range(4)]
                        stack.append((picked[0] + picked[1]) + (picked[2] + picked[3]))
            lines = jnp.dot(turn, jnp.concatenate(stack, 0), preferred_element_type=F32) + fill_ref[...]
            out_ref[pl.ds((qb * 64 + 32 * g) * LINES, 32 * LINES), :] = lines.astype(BF16)


def render(me, shear_pair, rate, slope, bias, live, target, owner, perm, brick):
    smem = pl.BlockSpec(memory_space=pltpu.SMEM)
    hbm = pl.BlockSpec(memory_space=pltpu.MemorySpace.HBM)
    return pl.pallas_call(
        render_kernel,
        in_specs=[smem] + [hbm] * 9,
        out_specs=pl.BlockSpec(memory_space=pltpu.VMEM),
        out_shape=jax.ShapeDtypeStruct((DEVICES * LINES, 128), BF16),
        scratch_shapes=[
            pltpu.SMEM((2,), F32),
            pltpu.SMEM((1, 1), F32),
            pltpu.SMEM((3,), F32),
            pltpu.SMEM((3,), F32),
            pltpu.SMEM((16,), jnp.int32),
            pltpu.SMEM((16,), jnp.int32),
            pltpu.SMEM((16,), jnp.int32),
            pltpu.VMEM((16, 16), jnp.int32),
            pltpu.VMEM((SAMPLES + 1, SIDE, SIDE), BF16),
            pltpu.VMEM((4, SIDE, SIDE), F32),
            pltpu.VMEM((STEP, RAYS, RAYS), F32),
            pltpu.VMEM((STEP, RAYS, RAYS), F32),
            pltpu.VMEM((RAYS, RAYS), F32),
            pltpu.VMEM((RAYS, RAYS), F32),
            pltpu.VMEM((3, RAYS, RAYS), F32),
            pltpu.VMEM((SIDE, SIDE), BF16),
            pltpu.VMEM((4, RAYS, RAYS), BF16),
            pltpu.VMEM((4, 2, RAYS, 128), BF16),
            pltpu.VMEM((32 * LINES, 128), F32),
            pltpu.SemaphoreType.DMA((BLOCKS,)),
            pltpu.SemaphoreType.DMA((8,)),
        ],
        cost_estimate=pl.CostEstimate(flops=4 * 10**9, transcendentals=50 * 10**6, bytes_accessed=5 * 10**6),
        name="render",
    )(me, shear_pair, rate, slope, bias, live, target, owner, perm, brick)


def composite_kernel(me_ref, owner_ref, view_ref, data_ref, out_ref, frag_ref, key_ref):
    at = iota((1, 16 * LINES), 1)
    from_slab = jnp.right_shift(at * 205, 11)
    line = at - LINES * from_slab
    spot = jnp.where(line < 8, from_slab * 8 + line, 128 + (line - 8) * 16 + from_slab)
    undo = ones_where(iota((16 * LINES, 16 * LINES), 0) == spot)
    keys = jnp.zeros((32, 128), F32)
    for i in range(GROUP):
        lines = data_ref[pl.ds(16 * LINES * i, 16 * LINES), :]
        lines = jnp.dot(undo, lines, preferred_element_type=F32)
        frag_ref[i] = lines[:128].reshape(GROUP, 8, 128)
        keys = keys + lines[128:]
    key_ref[...] = keys
    src = iota((RAYS, 128), 0)
    row_owner = bits(iota((128, 128), 0), 3, 15)
    flip = jnp.zeros((128, 128), jnp.int32)
    for t in range(16):
        flip = jnp.where(row_owner == owner_ref[t], view_ref[t], flip)
    flipped = jnp.concatenate([flip, flip], 0) == 1
    last = bits(3 + jnp.right_shift(me_ref[0], 2), 0, 3)
    lane = iota((1, RAYS), 1)
    channel = jnp.where(bits(lane, 4, 1) == 1, last, bits(lane, 5, 3))
    split = ones_where(iota((128, RAYS), 0) == channel * 32 + bits(lane, 7, 1) * 16 + bits(lane, 0, 15))
    row = iota((RAYS, 128), 0).astype(F32)

    def slab(d, carry):
        color, front = carry
        keys = [key_ref[pl.ds(16 * f2 + d, 1), :] for f2 in range(2)]
        data = frag_ref[:, d].reshape(128, 128).astype(BF16)
        value = jnp.dot(data, split, preferred_element_type=F32).astype(BF16)
        value = jnp.concatenate([value[:, :128], value[:, 128:]], 0)
        place = jnp.concatenate([ones_where(row == keys[f2]) for f2 in range(2)], 1)
        layer = jnp.dot(place, value, preferred_element_type=F32)
        clear = 1.0 - pltpu.roll(layer, 112, 1)
        color = jnp.where(flipped, layer + clear * color, color + front * layer)
        return color, front * clear

    start = (jnp.zeros((RAYS, 128), F32), jnp.ones((RAYS, 128), F32))
    color, front = lax.fori_loop(0, GROUP, slab, start, unroll=4)
    lane = iota((RAYS, 128), 1)
    final = jnp.where(bits(lane, 5, 3) == last, 1.0 - front, color)
    low = bits(iota((128, 128), 1), 4, 1) == 0
    final = jnp.where(low, final[:128], pltpu.roll(final[128:], 16, 1)).astype(BF16)
    out_ref[...] = jnp.broadcast_to(final.reshape(GROUP, 1, 8, 128), (GROUP, CHIPS, 8, 128))


def composite(me, owner, view, data):
    smem = pl.BlockSpec(memory_space=pltpu.SMEM)
    vmem = pl.BlockSpec(memory_space=pltpu.VMEM)
    return pl.pallas_call(
        composite_kernel,
        in_specs=[smem, smem, smem, vmem],
        out_specs=vmem,
        out_shape=jax.ShapeDtypeStruct((GROUP, CHIPS, 8, 128), BF16),
        scratch_shapes=[pltpu.VMEM((GROUP, GROUP, 8, 128), F32), pltpu.VMEM((32, 128), F32)],
        compiler_params=pltpu.CompilerParams(vmem_limit_bytes=VMEM_LIMIT),
        cost_estimate=pl.CostEstimate(flops=10**9, transcendentals=0, bytes_accessed=10**6),
        name="composite",
    )(me, owner, view, data)


def assemble_kernel(core_ref, mine_ref, other_ref, out_ref, wide_ref, spot_ref):
    at = iota((1, 128), 1)
    row = 2 * bits(at, 3, 7) + jnp.bitwise_xor(bits(at, 6, 1), core_ref[0])
    turn = ones_where(iota((128, 128), 0) == bits(at, 0, 7) * 16 + row)
    for qb in range(4):
        for g in range(4):
            at = pl.ds((qb * 4 + g) * 64, 64)
            lines = jnp.concatenate([mine_ref[at, :], other_ref[at, :]], 0)
            lines = jnp.dot(turn, lines, preferred_element_type=F32).astype(BF16)
            for pp in range(8):
                at = pl.ds(64 * (pp // 2) + 16 * g, 16)
                wide_ref[at, pl.ds((qb * 2 + pp % 2) * 128, 128)] = lines[16 * pp : 16 * pp + 16]
    src = iota((128, RAYS), 0)
    v = iota((1, RAYS), 1)
    block = bits(src, 0, 31)
    for qb in range(4):
        for pch in range(2):
            hit = (bits(v, 7, 1) == pch) & (bits(v, 4, 3) == qb)
            at = jnp.where(hit, 16 * bits(v, 6, 1) + bits(v, 0, 15), 32)
            spot_ref[pl.ds((qb * 2 + pch) * 128, 128), :] = ones_where(block == at)
    wide_lane = iota((16, 8 * 128), 1)
    lane_ch = bits(bits(wide_lane, 5, 3) - bits(wide_lane, 8, 3), 0, 3)
    for k in range(4):
        mask = jnp.concatenate([ones_where(lane_ch == k)] * 16, 0)
        out_ref[0, k] = jnp.dot(wide_ref[...] * mask, spot_ref[...], preferred_element_type=F32).astype(BF16)


def assemble(core, mine, other):
    vmem = pl.BlockSpec(memory_space=pltpu.VMEM)
    return pl.pallas_call(
        assemble_kernel,
        in_specs=[pl.BlockSpec(memory_space=pltpu.SMEM), vmem, vmem],
        out_specs=vmem,
        out_shape=jax.ShapeDtypeStruct((1, 4, RAYS, RAYS), BF16),
        scratch_shapes=[pltpu.VMEM((RAYS, 1024), BF16), pltpu.VMEM((1024, RAYS), BF16)],
        compiler_params=pltpu.CompilerParams(vmem_limit_bytes=VMEM_LIMIT),
        cost_estimate=pl.CostEstimate(flops=10**9, transcendentals=0, bytes_accessed=10**6),
        name="assemble",
    )(core, mine, other)


def exchange(blocks, axes):
    return lax.all_to_all(blocks, axes, split_axis=0, concat_axis=0, tiled=True)


def local(
    volume,
    shear,
    absorb,
    color_slope,
    color_bias,
    frag_tile,
    slot_perm,
    frag_rows,
    tile_view,
    tile_owner,
):
    me = lax.axis_index("tile").reshape(1)
    lines = render(
        me, shear[0, 0], absorb, color_slope, color_bias, frag_rows[0, 0],
        frag_tile.reshape(16), tile_owner, slot_perm[0, 0], volume[0, 0],
    )
    parts = exchange(lines.reshape(DEVICES, LINES // 2, 2, 128), ("tile", "chip", "core"))
    strips = composite(me, tile_owner, tile_view, parts.reshape(DEVICES * LINES, 128))
    mine = exchange(strips.reshape(GROUP * CHIPS, 8, 128), ("tile", "chip")).reshape(GROUP * CHIPS * 8, 128)
    other = lax.ppermute(mine, "core", ((0, 1), (1, 0)))
    return assemble(lax.axis_index("core").reshape(1), mine, other)


def solution(mesh):
    in_specs = (
        P("tile", ("chip", "core"), None, None, None),
        P("tile", ("chip", "core"), None),
        P("tile", ("chip", "core")),
        P(),
        P(),
        P("tile", ("chip", "core"), None, None),
        P("tile", ("chip", "core"), None, None),
        P("tile", ("chip", "core"), None),
        P(),
        P(),
    )
    out_specs = P("tile", None, None, None)
    mesh = Mesh(mesh.devices.reshape(GROUP, CHIPS, 2), ("tile", "chip", "core"))
    return jax.shard_map(local, mesh=mesh, in_specs=in_specs, out_specs=out_specs, check_vma=False)
```

```python
import math
import jax
import jax.numpy as jnp
import numpy as np
from jax import lax
from jax.experimental import pallas as pl
from jax.experimental.pallas import tpu as pltpu
from jax.sharding import Mesh, PartitionSpec as P

SAMPLES = 128
RAYS = 256
SIDE = 128
STEP = 8
BLOCKS = SAMPLES // STEP
ROWS = RAYS // STEP
LOG2E = math.log2(math.e)
GROUP = 16
DEVICES = 256
CHIPS = 8
LINES = 10
TOGETHER = 4
VMEM_LIMIT = 48 * 2**20
F32 = jnp.float32
BF16 = jnp.bfloat16


def iota(shape, dim):
    return lax.broadcasted_iota(jnp.int32, shape, dim)


def bits(value, shift, mask):
    return jnp.bitwise_and(jnp.right_shift(value, shift), mask)


def ones_where(condition):
    return jnp.where(condition, 1.0, 0.0).astype(BF16)


def spline(offset):
    size_abs = jnp.abs(offset)
    inner = 2.0 / 3.0 - size_abs * size_abs + 0.5 * size_abs * size_abs * size_abs
    remain = 2.0 - size_abs
    outer = remain * remain * remain / 6.0
    return jnp.where(size_abs < 1.0, inner, jnp.where(size_abs < 2.0, outer, 0.0))


def wrapped(diff):
    return jnp.bitwise_and(diff + 64, 127) - 64


def band(base, mask_ref):
    base = jnp.concatenate([base, pltpu.roll(base, 8, 1)], 0).astype(BF16)
    parts = []
    for k in range(SIDE // 16):
        part = pltpu.roll(base, 16 * k, 1) if k else base
        if k not in (3, 4):
            part = part * mask_ref[pl.ds(16 * k, 16), :]
        parts.append(part)
    return jnp.concatenate(parts, 0)


def key_lines(me, target_ref, owner_ref, perm):
    frag = iota((16, 16), 0)
    tile = iota((16, 16), 1)
    target = jnp.zeros((16, 16), jnp.int32)
    owners = jnp.zeros((16, 16), jnp.int32)
    for t in range(16):
        target = jnp.where(frag == t, target_ref[t], target)
        owners = jnp.where(tile == t, owner_ref[t], owners)
    onehot = jnp.where(target == tile, 1.0, 0.0)
    earlier = jnp.where(tile < frag, 1.0, 0.0)
    ahead = jnp.dot(earlier, onehot, preferred_element_type=F32)
    rank = jnp.sum(ahead * onehot, 1, keepdims=True)
    spots = jnp.dot(onehot, perm.astype(F32), preferred_element_type=F32)
    position = jnp.sum(jnp.where(tile.astype(F32) == rank, spots, 0.0), 1, keepdims=True).astype(jnp.int32)
    owner = jnp.sum(onehot * owners.astype(F32), 1, keepdims=True).astype(jnp.int32)
    key = bits(position, 0, 1) * 128 + owner * 8 + bits(position, 1, 7)
    key = jnp.broadcast_to(key, (16, 128)).astype(F32)
    f = iota((16, 128), 0)
    here = iota((16, 128), 1) == me * 8 + bits(f, 1, 7)
    return [jnp.sum(jnp.where(here & (bits(f, 0, 1) == f2), key, 0.0), 0, keepdims=True) for f2 in range(2)]


def render_kernel(
    me_ref, shear_hbm, rate_hbm, slope_hbm, bias_hbm, live_hbm, target_hbm, owner_hbm, perm_hbm, vol_hbm, out_ref,
    shear_ref, rate_ref, slope_ref, bias_ref, live_ref, target_ref, owner_ref, perm_ref,
    vol_ref, wide_ref, even_ref, odd_ref, cum_ref, clear_ref, acc_ref, mask_ref, plane_ref, pick_ref, fill_ref,
    sems, small_sems,
):
    small = (
        (shear_hbm, shear_ref), (rate_hbm, rate_ref), (slope_hbm, slope_ref), (bias_hbm, bias_ref),
        (live_hbm, live_ref), (target_hbm, target_ref), (owner_hbm, owner_ref), (perm_hbm, perm_ref),
    )
    small = [pltpu.make_async_copy(src, dst, small_sems.at[k]) for k, (src, dst) in enumerate(small)]
    for copy in small:
        copy.start()
    w0 = LOG2E * float(np.float32(2.0 / 3.0).astype(BF16))
    w1 = LOG2E * float(np.float32(1.0 / 6.0).astype(BF16))

    def chunk(k):
        at = pl.ds(k * STEP, STEP)
        return pltpu.make_async_copy(vol_hbm.at[at], vol_ref.at[at], sems.at[k])

    for k in range(BLOCKS):
        chunk(k).start()
    r = iota((SIDE, SIDE), 0)
    c = iota((SIDE, SIDE), 1)
    mask_ref[...] = ones_where(jnp.abs(r - c) < 64)
    cum_ref[...] = jnp.zeros_like(cum_ref)
    clear_ref[...] = jnp.ones_like(clear_ref)
    acc_ref[...] = jnp.zeros_like(acc_ref)
    wide_ref[3] = jnp.zeros((SIDE, SIDE), F32)
    vol_ref[SAMPLES] = jnp.zeros((SIDE, SIDE), BF16)
    for copy in small:
        copy.wait()
    key = key_lines(me_ref[0], target_ref, owner_ref, perm_ref[...])
    from_line = jnp.where(bits(iota((64, 128), 0), 0, 1) == 0, key[0], key[1]).astype(BF16)
    at = iota((1, 64), 1)
    spots = ones_where(iota((32 * LINES, 64), 0) == bits(at, 1, 31) * LINES + 8 + bits(at, 0, 1))
    fill_ref[...] = jnp.dot(spots, from_line, preferred_element_type=F32)
    chunk(0).wait()
    wide_ref[0] = vol_ref[0].astype(F32)

    def make_field(field_ref, block, j):
        s = block * STEP + j
        centred = s.astype(F32) - (SIDE - 1) / 2.0
        before = wide_ref[jnp.bitwise_and(s + 3, 3)]
        here = wide_ref[jnp.bitwise_and(s, 3)]
        after = vol_ref[jnp.minimum(s + 1, SAMPLES)].astype(F32)
        wide_ref[jnp.bitwise_and(s + 1, 3)] = after
        cells = (w0 * here + w1 * (before + after)).astype(BF16)
        i = iota((8, SIDE), 0)
        a = iota((8, SIDE), 1)
        d_row = wrapped(i - a).astype(F32)
        d_col = wrapped(a - i).astype(F32)
        shift_r = shear_ref[0] * centred
        shift_c = shear_ref[1] * centred
        rows = jnp.concatenate([band(spline(d_row + (shift_r + q)), mask_ref) for q in (-0.25, 0.25)], 0)
        cols = jnp.concatenate([band(spline(d_col + (shift_c + q)), mask_ref) for q in (-0.25, 0.25)], 1)
        half = jnp.dot(rows, cells, preferred_element_type=F32).astype(BF16)
        field_ref[j] = jnp.dot(half, cols, preferred_element_type=F32)

    def integrate(field_ref, r):
        neg_rate = -rate_ref[0, 0]
        for part in range(2 * (ROWS // 16)):
            sub, side = part // 2, pl.ds(128 * (part % 2), 128)
            at = pl.ds(pl.multiple_of(r * ROWS + 16 * sub, 16), 16)
            cum = cum_ref[at, side]
            clear = clear_ref[at, side]
            terms = [[], [], []]
            for j in range(STEP):
                f = field_ref[j, at, side]
                cum = cum + lax.log2(1.0 + jnp.exp2(f))
                after = jnp.exp2(neg_rate * cum)
                w = (clear - after).astype(BF16)
                clear = after
                f = f.astype(BF16)
                for k in range(3):
                    terms[k].append(w * jnp.tanh(f * slopes[k][j % 4] + biases[k][j % 4]))
                    size = 1
                    while (j + 1) % (2 * size) == 0:
                        last = terms[k].pop()
                        terms[k][-1] = terms[k][-1] + last
                        size *= 2
            cum_ref[at, side] = cum
            clear_ref[at, side] = clear
            for k in range(3):
                acc_ref[k, at, side] += terms[k][0].astype(F32)

    def rounded(value):
        want, have, parts = jnp.full((16, 128), value, F32), jnp.zeros((16, 128), F32), []
        for n in range(4):
            parts.append(((n + 1) * want - have).astype(BF16))
            have = have + parts[-1].astype(F32)
        return parts

    slopes = [rounded((0.5 / LOG2E) * slope_ref[k]) for k in range(3)]
    biases = [rounded(0.5 * bias_ref[k]) for k in range(3)]

    def every(body):
        @pl.loop(0, STEP // TOGETHER)
        def _(r):
            for i in range(TOGETHER):
                body(TOGETHER * r + i)

    def fused(made_ref, used_ref, block):
        @pl.when(block + 1 < BLOCKS)
        def _():
            chunk(jnp.minimum(block + 1, BLOCKS - 1)).wait()

        def both(r):
            integrate(used_ref, r)
            make_field(made_ref, block, r)

        every(both)

    chunk(1).wait()
    every(lambda r: make_field(even_ref, 0, r))

    @pl.loop(0, BLOCKS // 2)
    def _(t):
        fused(odd_ref, even_ref, 2 * t + 1)
        fused(even_ref, odd_ref, 2 * t + 2)

    col = iota((8, RAYS), 1)
    lane_fv = bits(col, 5, 3)
    alpha = 1.0 - clear_ref[...]
    for k in range(4):
        plane_ref[k] = (alpha if k == 3 else 0.5 * (alpha + acc_ref[k])).astype(BF16)
    for fu in range(4):
        limit = jnp.zeros((8, RAYS), jnp.int32)
        for fv in range(4):
            limit = jnp.where(lane_fv == fv, live_ref[4 * fu + fv], limit)
        limit = jnp.concatenate([limit] * 4, 0)
        for par in range(2):
            at = pl.ds(128 * par + 32 * fu, 32)
            keep = ones_where(2 * iota((32, RAYS), 0) + par < limit)
            for k in range(4):
                plane_ref[k, at, :] = plane_ref[k, at, :] * keep
    lane = iota((1, RAYS), 1)
    src = iota((RAYS, RAYS), 0)
    for k in range(4):
        v = 128 * bits(lane, 7, 1) + 64 * bits(lane, 4, 1) + 16 * bits(bits(lane, 5, 3) - k, 0, 3) + bits(lane, 0, 15)
        select = ones_where(src == bits(v, 0, 1) * 128 + bits(v, 1, 127))
        got = jnp.dot(plane_ref[k], select, preferred_element_type=F32).astype(BF16)
        for fvh in range(2):
            pick_ref[k, fvh] = got[:, 128 * fvh : 128 * fvh + 128]
    spot = (bits(lane, 0, 15) * 2 + bits(lane, 4, 1)) * LINES + bits(lane, 5, 7)
    turn = ones_where(iota((32 * LINES, RAYS), 0) == spot)
    block = bits(iota((16, 128), 1), 5, 3)
    for qb in range(4):
        masks = [ones_where(block == (k + qb) % 4) for k in range(4)]
        for g in range(2):
            stack = []
            for fu in range(4):
                for fvh in range(2):
                    for par in range(2):
                        at = pl.ds(128 * par + 32 * fu + 16 * g, 16)
                        picked = [pick_ref[k, fvh, at, :] * masks[k] for k in range(4)]
                        stack.append((picked[0] + picked[1]) + (picked[2] + picked[3]))
            lines = jnp.dot(turn, jnp.concatenate(stack, 0), preferred_element_type=F32) + fill_ref[...]
            out_ref[pl.ds((qb * 64 + 32 * g) * LINES, 32 * LINES), :] = lines.astype(BF16)


def render(me, shear_pair, rate, slope, bias, live, target, owner, perm, brick):
    smem = pl.BlockSpec(memory_space=pltpu.SMEM)
    hbm = pl.BlockSpec(memory_space=pltpu.MemorySpace.HBM)
    return pl.pallas_call(
        render_kernel,
        in_specs=[smem] + [hbm] * 9,
        out_specs=pl.BlockSpec(memory_space=pltpu.VMEM),
        out_shape=jax.ShapeDtypeStruct((DEVICES * LINES, 128), BF16),
        scratch_shapes=[
            pltpu.SMEM((2,), F32),
            pltpu.SMEM((1, 1), F32),
            pltpu.SMEM((3,), F32),
            pltpu.SMEM((3,), F32),
            pltpu.SMEM((16,), jnp.int32),
            pltpu.SMEM((16,), jnp.int32),
            pltpu.SMEM((16,), jnp.int32),
            pltpu.VMEM((16, 16), jnp.int32),
            pltpu.VMEM((SAMPLES + 1, SIDE, SIDE), BF16),
            pltpu.VMEM((4, SIDE, SIDE), F32),
            pltpu.VMEM((STEP, RAYS, RAYS), F32),
            pltpu.VMEM((STEP, RAYS, RAYS), F32),
            pltpu.VMEM((RAYS, RAYS), F32),
            pltpu.VMEM((RAYS, RAYS), F32),
            pltpu.VMEM((3, RAYS, RAYS), F32),
            pltpu.VMEM((SIDE, SIDE), BF16),
            pltpu.VMEM((4, RAYS, RAYS), BF16),
            pltpu.VMEM((4, 2, RAYS, 128), BF16),
            pltpu.VMEM((32 * LINES, 128), F32),
            pltpu.SemaphoreType.DMA((BLOCKS,)),
            pltpu.SemaphoreType.DMA((8,)),
        ],
        cost_estimate=pl.CostEstimate(flops=4 * 10**9, transcendentals=50 * 10**6, bytes_accessed=5 * 10**6),
        name="render",
    )(me, shear_pair, rate, slope, bias, live, target, owner, perm, brick)


def composite_kernel(me_ref, owner_ref, view_ref, data_ref, out_ref, frag_ref, key_ref):
    at = iota((1, 16 * LINES), 1)
    from_slab = jnp.right_shift(at * 205, 11)
    line = at - LINES * from_slab
    spot = jnp.where(line < 8, from_slab * 8 + line, 128 + (line - 8) * 16 + from_slab)
    undo = ones_where(iota((16 * LINES, 16 * LINES), 0) == spot)
    keys = jnp.zeros((32, 128), F32)
    for i in range(GROUP):
        lines = data_ref[pl.ds(16 * LINES * i, 16 * LINES), :]
        lines = jnp.dot(undo, lines, preferred_element_type=F32)
        frag_ref[i] = lines[:128].reshape(GROUP, 8, 128)
        keys = keys + lines[128:]
    key_ref[...] = keys
    src = iota((RAYS, 128), 0)
    row_owner = bits(iota((128, 128), 0), 3, 15)
    flip = jnp.zeros((128, 128), jnp.int32)
    for t in range(16):
        flip = jnp.where(row_owner == owner_ref[t], view_ref[t], flip)
    flipped = jnp.concatenate([flip, flip], 0) == 1
    last = bits(3 + jnp.right_shift(me_ref[0], 2), 0, 3)
    lane = iota((1, RAYS), 1)
    channel = jnp.where(bits(lane, 4, 1) == 1, last, bits(lane, 5, 3))
    split = ones_where(iota((128, RAYS), 0) == channel * 32 + bits(lane, 7, 1) * 16 + bits(lane, 0, 15))
    row = iota((RAYS, 128), 0).astype(F32)

    def slab(d, carry):
        color, front = carry
        keys = [key_ref[pl.ds(16 * f2 + d, 1), :] for f2 in range(2)]
        data = frag_ref[:, d].reshape(128, 128).astype(BF16)
        value = jnp.dot(data, split, preferred_element_type=F32).astype(BF16)
        value = jnp.concatenate([value[:, :128], value[:, 128:]], 0)
        place = jnp.concatenate([ones_where(row == keys[f2]) for f2 in range(2)], 1)
        layer = jnp.dot(place, value, preferred_element_type=F32)
        clear = 1.0 - pltpu.roll(layer, 112, 1)
        color = jnp.where(flipped, layer + clear * color, color + front * layer)
        return color, front * clear

    start = (jnp.zeros((RAYS, 128), F32), jnp.ones((RAYS, 128), F32))
    color, front = lax.fori_loop(0, GROUP, slab, start, unroll=4)
    lane = iota((RAYS, 128), 1)
    final = jnp.where(bits(lane, 5, 3) == last, 1.0 - front, color)
    low = bits(iota((128, 128), 1), 4, 1) == 0
    final = jnp.where(low, final[:128], pltpu.roll(final[128:], 16, 1)).astype(BF16)
    out_ref[...] = jnp.broadcast_to(final.reshape(GROUP, 1, 8, 128), (GROUP, CHIPS, 8, 128))


def composite(me, owner, view, data):
    smem = pl.BlockSpec(memory_space=pltpu.SMEM)
    vmem = pl.BlockSpec(memory_space=pltpu.VMEM)
    return pl.pallas_call(
        composite_kernel,
        in_specs=[smem, smem, smem, vmem],
        out_specs=vmem,
        out_shape=jax.ShapeDtypeStruct((GROUP, CHIPS, 8, 128), BF16),
        scratch_shapes=[pltpu.VMEM((GROUP, GROUP, 8, 128), F32), pltpu.VMEM((32, 128), F32)],
        compiler_params=pltpu.CompilerParams(vmem_limit_bytes=VMEM_LIMIT),
        cost_estimate=pl.CostEstimate(flops=10**9, transcendentals=0, bytes_accessed=10**6),
        name="composite",
    )(me, owner, view, data)


def assemble_kernel(core_ref, mine_ref, other_ref, out_ref, wide_ref):
    at = iota((1, 128), 1)
    row = 2 * bits(at, 3, 7) + jnp.bitwise_xor(bits(at, 6, 1), core_ref[0])
    turn = ones_where(iota((128, 128), 0) == bits(at, 0, 7) * 16 + row)
    for qb in range(4):
        for g in range(4):
            at = pl.ds((qb * 4 + g) * 64, 64)
            lines = jnp.concatenate([mine_ref[at, :], other_ref[at, :]], 0)
            lines = jnp.dot(turn, lines, preferred_element_type=F32)
            for pp in range(8):
                wide_ref[qb, pp % 2, pl.ds(64 * (pp // 2) + 16 * g, 16), :] = lines[16 * pp : 16 * pp + 16]
    block = bits(iota((RAYS, 128), 1), 5, 3)
    src = iota((RAYS, RAYS), 0)
    v = iota((1, RAYS), 1)
    for k in range(4):
        parts = []
        for pch in range(2):
            part = wide_ref[0, pch]
            for qb in range(1, 4):
                part = jnp.where(block == (k + qb) % 4, wide_ref[qb, pch], part)
            parts.append(part.astype(BF16))
        at = 128 * bits(v, 7, 1) + 32 * bits(k + bits(v, 4, 3), 0, 3) + 16 * bits(v, 6, 1) + bits(v, 0, 15)
        out_ref[0, k] = jnp.dot(
            jnp.concatenate(parts, 1), ones_where(src == at), preferred_element_type=F32
        ).astype(BF16)


def assemble(core, mine, other):
    vmem = pl.BlockSpec(memory_space=pltpu.VMEM)
    return pl.pallas_call(
        assemble_kernel,
        in_specs=[pl.BlockSpec(memory_space=pltpu.SMEM), vmem, vmem],
        out_specs=vmem,
        out_shape=jax.ShapeDtypeStruct((1, 4, RAYS, RAYS), BF16),
        scratch_shapes=[pltpu.VMEM((4, 2, RAYS, 128), F32)],
        compiler_params=pltpu.CompilerParams(vmem_limit_bytes=VMEM_LIMIT),
        cost_estimate=pl.CostEstimate(flops=10**9, transcendentals=0, bytes_accessed=10**6),
        name="assemble",
    )(core, mine, other)


def exchange(blocks, axes):
    return lax.all_to_all(blocks, axes, split_axis=0, concat_axis=0, tiled=True)


def local(
    volume,
    shear,
    absorb,
    color_slope,
    color_bias,
    frag_tile,
    slot_perm,
    frag_rows,
    tile_view,
    tile_owner,
):
    me = lax.axis_index("tile").reshape(1)
    lines = render(
        me, shear[0, 0], absorb, color_slope, color_bias, frag_rows[0, 0],
        frag_tile.reshape(16), tile_owner, slot_perm[0, 0], volume[0, 0],
    )
    parts = exchange(lines.reshape(DEVICES, LINES // 2, 2, 128), ("tile", "chip", "core"))
    strips = composite(me, tile_owner, tile_view, parts.reshape(DEVICES * LINES, 128))
    mine = exchange(strips.reshape(GROUP * CHIPS, 8, 128), ("tile", "chip")).reshape(GROUP * CHIPS * 8, 128)
    other = lax.ppermute(mine, "core", ((0, 1), (1, 0)))
    return assemble(lax.axis_index("core").reshape(1), mine, other)


def solution(mesh):
    in_specs = (
        P("tile", ("chip", "core"), None, None, None),
        P("tile", ("chip", "core"), None),
        P("tile", ("chip", "core")),
        P(),
        P(),
        P("tile", ("chip", "core"), None, None),
        P("tile", ("chip", "core"), None, None),
        P("tile", ("chip", "core"), None),
        P(),
        P(),
    )
    out_specs = P("tile", None, None, None)
    mesh = Mesh(mesh.devices.reshape(GROUP, CHIPS, 2), ("tile", "chip", "core"))
    return jax.shard_map(local, mesh=mesh, in_specs=in_specs, out_specs=out_specs, check_vma=False)
```

```python
import math
import jax
import jax.numpy as jnp
import numpy as np
from jax import lax
from jax.experimental import pallas as pl
from jax.experimental.pallas import tpu as pltpu
from jax.sharding import Mesh, PartitionSpec as P

SAMPLES = 128
RAYS = 256
SIDE = 128
STEP = 8
BLOCKS = SAMPLES // STEP
ROWS = RAYS // STEP
LOG2E = math.log2(math.e)
GROUP = 16
DEVICES = 256
CHIPS = 8
LINES = 10
TOGETHER = 4
VMEM_LIMIT = 48 * 2**20
F32 = jnp.float32
BF16 = jnp.bfloat16


def iota(shape, dim):
    return lax.broadcasted_iota(jnp.int32, shape, dim)


def bits(value, shift, mask):
    return jnp.bitwise_and(jnp.right_shift(value, shift), mask)


def ones_where(condition):
    return jnp.where(condition, 1.0, 0.0).astype(BF16)


def spline(offset):
    size_abs = jnp.abs(offset)
    inner = 2.0 / 3.0 - size_abs * size_abs + 0.5 * size_abs * size_abs * size_abs
    remain = 2.0 - size_abs
    outer = remain * remain * remain / 6.0
    return jnp.where(size_abs < 1.0, inner, jnp.where(size_abs < 2.0, outer, 0.0))


def wrapped(diff):
    return jnp.bitwise_and(diff + 64, 127) - 64


def band(base, mask_ref):
    base = jnp.concatenate([base, pltpu.roll(base, 8, 1)], 0).astype(BF16)
    parts = []
    for k in range(SIDE // 16):
        part = pltpu.roll(base, 16 * k, 1) if k else base
        if k not in (3, 4):
            part = part * mask_ref[pl.ds(16 * k, 16), :]
        parts.append(part)
    return jnp.concatenate(parts, 0)


def key_lines(me, target_ref, owner_ref, perm):
    frag = iota((16, 16), 0)
    tile = iota((16, 16), 1)
    target = jnp.zeros((16, 16), jnp.int32)
    owners = jnp.zeros((16, 16), jnp.int32)
    for t in range(16):
        target = jnp.where(frag == t, target_ref[t], target)
        owners = jnp.where(tile == t, owner_ref[t], owners)
    onehot = jnp.where(target == tile, 1.0, 0.0)
    earlier = jnp.where(tile < frag, 1.0, 0.0)
    ahead = jnp.dot(earlier, onehot, preferred_element_type=F32)
    rank = jnp.sum(ahead * onehot, 1, keepdims=True)
    spots = jnp.dot(onehot, perm.astype(F32), preferred_element_type=F32)
    position = jnp.sum(jnp.where(tile.astype(F32) == rank, spots, 0.0), 1, keepdims=True).astype(jnp.int32)
    owner = jnp.sum(onehot * owners.astype(F32), 1, keepdims=True).astype(jnp.int32)
    key = bits(position, 0, 1) * 128 + owner * 8 + bits(position, 1, 7)
    key = jnp.broadcast_to(key, (16, 128)).astype(F32)
    f = iota((16, 128), 0)
    here = iota((16, 128), 1) == me * 8 + bits(f, 1, 7)
    return [jnp.sum(jnp.where(here & (bits(f, 0, 1) == f2), key, 0.0), 0, keepdims=True) for f2 in range(2)]


def render_kernel(
    me_ref, shear_hbm, rate_hbm, slope_hbm, bias_hbm, live_hbm, target_hbm, owner_hbm, perm_hbm, vol_hbm, out_ref,
    shear_ref, rate_ref, slope_ref, bias_ref, live_ref, target_ref, owner_ref, perm_ref,
    vol_ref, wide_ref, even_ref, odd_ref, cum_ref, clear_ref, acc_ref, mask_ref, plane_ref, pick_ref, fill_ref,
    sems, small_sems,
):
    small = (
        (shear_hbm, shear_ref), (rate_hbm, rate_ref), (slope_hbm, slope_ref), (bias_hbm, bias_ref),
        (live_hbm, live_ref), (target_hbm, target_ref), (owner_hbm, owner_ref), (perm_hbm, perm_ref),
    )
    small = [pltpu.make_async_copy(src, dst, small_sems.at[k]) for k, (src, dst) in enumerate(small)]
    for copy in small:
        copy.start()
    w0 = LOG2E * float(np.float32(2.0 / 3.0).astype(BF16))
    w1 = LOG2E * float(np.float32(1.0 / 6.0).astype(BF16))

    def chunk(k):
        at = pl.ds(k * STEP, STEP)
        return pltpu.make_async_copy(vol_hbm.at[at], vol_ref.at[at], sems.at[k])

    for k in range(BLOCKS):
        chunk(k).start()
    r = iota((SIDE, SIDE), 0)
    c = iota((SIDE, SIDE), 1)
    mask_ref[...] = ones_where(jnp.abs(r - c) < 64)
    cum_ref[...] = jnp.zeros_like(cum_ref)
    clear_ref[...] = jnp.ones_like(clear_ref)
    acc_ref[...] = jnp.zeros_like(acc_ref)
    wide_ref[3] = jnp.zeros((SIDE, SIDE), F32)
    vol_ref[SAMPLES] = jnp.zeros((SIDE, SIDE), BF16)
    for copy in small:
        copy.wait()
    key = key_lines(me_ref[0], target_ref, owner_ref, perm_ref[...])
    from_line = jnp.where(bits(iota((64, 128), 0), 0, 1) == 0, key[0], key[1]).astype(BF16)
    at = iota((1, 64), 1)
    spots = ones_where(iota((32 * LINES, 64), 0) == bits(at, 1, 31) * LINES + 8 + bits(at, 0, 1))
    fill_ref[...] = jnp.dot(spots, from_line, preferred_element_type=F32)
    chunk(0).wait()
    wide_ref[0] = vol_ref[0].astype(F32)

    def make_field(field_ref, block, j):
        s = block * STEP + j
        centred = s.astype(F32) - (SIDE - 1) / 2.0
        before = wide_ref[jnp.bitwise_and(s + 3, 3)]
        here = wide_ref[jnp.bitwise_and(s, 3)]
        after = vol_ref[jnp.minimum(s + 1, SAMPLES)].astype(F32)
        wide_ref[jnp.bitwise_and(s + 1, 3)] = after
        cells = (w0 * here + w1 * (before + after)).astype(BF16)
        i = iota((8, SIDE), 0)
        a = iota((8, SIDE), 1)
        d_row = wrapped(i - a).astype(F32)
        d_col = wrapped(a - i).astype(F32)
        shift_r = shear_ref[0] * centred
        shift_c = shear_ref[1] * centred
        rows = jnp.concatenate([band(spline(d_row + (shift_r + q)), mask_ref) for q in (-0.25, 0.25)], 0)
        cols = jnp.concatenate([band(spline(d_col + (shift_c + q)), mask_ref) for q in (-0.25, 0.25)], 1)
        half = jnp.dot(rows, cells, preferred_element_type=F32).astype(BF16)
        field_ref[j] = jnp.dot(half, cols, preferred_element_type=F32)

    def integrate(field_ref, r):
        neg_rate = -rate_ref[0, 0]
        for part in range(2 * (ROWS // 16)):
            sub, side = part // 2, pl.ds(128 * (part % 2), 128)
            at = pl.ds(pl.multiple_of(r * ROWS + 16 * sub, 16), 16)
            cum = cum_ref[at, side]
            clear = clear_ref[at, side]
            terms = [[], [], []]
            for j in range(STEP):
                f = field_ref[j, at, side]
                cum = cum + lax.log2(1.0 + jnp.exp2(f))
                after = jnp.exp2(neg_rate * cum)
                w = (clear - after).astype(BF16)
                clear = after
                f = f.astype(BF16)
                for k in range(3):
                    terms[k].append(w * jnp.tanh(f * slopes[k][j % 2] + biases[k][j % 2]))
                    size = 1
                    while (j + 1) % (2 * size) == 0:
                        last = terms[k].pop()
                        terms[k][-1] = terms[k][-1] + last
                        size *= 2
            cum_ref[at, side] = cum
            clear_ref[at, side] = clear
            for k in range(3):
                acc_ref[k, at, side] += terms[k][0].astype(F32)

    def rounded(value):
        want, have, parts = jnp.full((16, 128), value, F32), jnp.zeros((16, 128), F32), []
        for n in range(2):
            parts.append(((n + 1) * want - have).astype(BF16))
            have = have + parts[-1].astype(F32)
        return parts

    slopes = [rounded((0.5 / LOG2E) * slope_ref[k]) for k in range(3)]
    biases = [rounded(0.5 * bias_ref[k]) for k in range(3)]

    def every(body):
        @pl.loop(0, STEP // TOGETHER)
        def _(r):
            for i in range(TOGETHER):
                body(TOGETHER * r + i)

    def fused(made_ref, used_ref, block):
        @pl.when(block + 1 < BLOCKS)
        def _():
            chunk(jnp.minimum(block + 1, BLOCKS - 1)).wait()

        def both(r):
            integrate(used_ref, r)
            make_field(made_ref, block, r)

        every(both)

    chunk(1).wait()
    every(lambda r: make_field(even_ref, 0, r))

    @pl.loop(0, BLOCKS // 2)
    def _(t):
        fused(odd_ref, even_ref, 2 * t + 1)

        @pl.when(t < BLOCKS // 2 - 1)
        def _():
            fused(even_ref, odd_ref, 2 * t + 2)

    every(lambda r: integrate(odd_ref, r))

    col = iota((8, RAYS), 1)
    lane_fv = bits(col, 5, 3)
    alpha = 1.0 - clear_ref[...]
    for k in range(4):
        plane_ref[k] = (alpha if k == 3 else 0.5 * (alpha + acc_ref[k])).astype(BF16)
    for fu in range(4):
        limit = jnp.zeros((8, RAYS), jnp.int32)
        for fv in range(4):
            limit = jnp.where(lane_fv == fv, live_ref[4 * fu + fv], limit)
        limit = jnp.concatenate([limit] * 4, 0)
        for par in range(2):
            at = pl.ds(128 * par + 32 * fu, 32)
            keep = ones_where(2 * iota((32, RAYS), 0) + par < limit)
            for k in range(4):
                plane_ref[k, at, :] = plane_ref[k, at, :] * keep
    lane = iota((1, RAYS), 1)
    src = iota((RAYS, RAYS), 0)
    for k in range(4):
        v = 128 * bits(lane, 7, 1) + 64 * bits(lane, 4, 1) + 16 * bits(bits(lane, 5, 3) - k, 0, 3) + bits(lane, 0, 15)
        select = ones_where(src == bits(v, 0, 1) * 128 + bits(v, 1, 127))
        got = jnp.dot(plane_ref[k], select, preferred_element_type=F32).astype(BF16)
        for fvh in range(2):
            pick_ref[k, fvh] = got[:, 128 * fvh : 128 * fvh + 128]
    spot = (bits(lane, 0, 15) * 2 + bits(lane, 4, 1)) * LINES + bits(lane, 5, 7)
    turn = ones_where(iota((32 * LINES, RAYS), 0) == spot)
    block = bits(iota((16, 128), 1), 5, 3)
    for qb in range(4):
        masks = [ones_where(block == (k + qb) % 4) for k in range(4)]
        for g in range(2):
            stack = []
            for fu in range(4):
                for fvh in range(2):
                    for par in range(2):
                        at = pl.ds(128 * par + 32 * fu + 16 * g, 16)
                        picked = [pick_ref[k, fvh, at, :] * masks[k] for k in range(4)]
                        stack.append((picked[0] + picked[1]) + (picked[2] + picked[3]))
            lines = jnp.dot(turn, jnp.concatenate(stack, 0), preferred_element_type=F32) + fill_ref[...]
            out_ref[pl.ds((qb * 64 + 32 * g) * LINES, 32 * LINES), :] = lines.astype(BF16)


def render(me, shear_pair, rate, slope, bias, live, target, owner, perm, brick):
    smem = pl.BlockSpec(memory_space=pltpu.SMEM)
    hbm = pl.BlockSpec(memory_space=pltpu.MemorySpace.HBM)
    return pl.pallas_call(
        render_kernel,
        in_specs=[smem] + [hbm] * 9,
        out_specs=pl.BlockSpec(memory_space=pltpu.VMEM),
        out_shape=jax.ShapeDtypeStruct((DEVICES * LINES, 128), BF16),
        scratch_shapes=[
            pltpu.SMEM((2,), F32),
            pltpu.SMEM((1, 1), F32),
            pltpu.SMEM((3,), F32),
            pltpu.SMEM((3,), F32),
            pltpu.SMEM((16,), jnp.int32),
            pltpu.SMEM((16,), jnp.int32),
            pltpu.SMEM((16,), jnp.int32),
            pltpu.VMEM((16, 16), jnp.int32),
            pltpu.VMEM((SAMPLES + 1, SIDE, SIDE), BF16),
            pltpu.VMEM((4, SIDE, SIDE), F32),
            pltpu.VMEM((STEP, RAYS, RAYS), F32),
            pltpu.VMEM((STEP, RAYS, RAYS), F32),
            pltpu.VMEM((RAYS, RAYS), F32),
            pltpu.VMEM((RAYS, RAYS), F32),
            pltpu.VMEM((3, RAYS, RAYS), F32),
            pltpu.VMEM((SIDE, SIDE), BF16),
            pltpu.VMEM((4, RAYS, RAYS), BF16),
            pltpu.VMEM((4, 2, RAYS, 128), BF16),
            pltpu.VMEM((32 * LINES, 128), F32),
            pltpu.SemaphoreType.DMA((BLOCKS,)),
            pltpu.SemaphoreType.DMA((8,)),
        ],
        cost_estimate=pl.CostEstimate(flops=4 * 10**9, transcendentals=50 * 10**6, bytes_accessed=5 * 10**6),
        name="render",
    )(me, shear_pair, rate, slope, bias, live, target, owner, perm, brick)


def composite_kernel(me_ref, owner_ref, view_ref, data_ref, out_ref, frag_ref, key_ref):
    at = iota((1, 16 * LINES), 1)
    from_slab = jnp.right_shift(at * 205, 11)
    line = at - LINES * from_slab
    spot = jnp.where(line < 8, from_slab * 8 + line, 128 + (line - 8) * 16 + from_slab)
    undo = ones_where(iota((16 * LINES, 16 * LINES), 0) == spot)
    keys = jnp.zeros((32, 128), F32)
    for i in range(GROUP):
        lines = data_ref[pl.ds(16 * LINES * i, 16 * LINES), :]
        lines = jnp.dot(undo, lines, preferred_element_type=F32)
        frag_ref[i] = lines[:128].reshape(GROUP, 8, 128)
        keys = keys + lines[128:]
    key_ref[...] = keys
    src = iota((RAYS, 128), 0)
    row_owner = bits(iota((128, 128), 0), 3, 15)
    flip = jnp.zeros((128, 128), jnp.int32)
    for t in range(16):
        flip = jnp.where(row_owner == owner_ref[t], view_ref[t], flip)
    flipped = jnp.concatenate([flip, flip], 0) == 1
    last = bits(3 + jnp.right_shift(me_ref[0], 2), 0, 3)
    lane = iota((1, RAYS), 1)
    channel = jnp.where(bits(lane, 4, 1) == 1, last, bits(lane, 5, 3))
    split = ones_where(iota((128, RAYS), 0) == channel * 32 + bits(lane, 7, 1) * 16 + bits(lane, 0, 15))
    row = iota((RAYS, 128), 0).astype(F32)

    def slab(d, carry):
        color, front = carry
        keys = [key_ref[pl.ds(16 * f2 + d, 1), :] for f2 in range(2)]
        data = frag_ref[:, d].reshape(128, 128).astype(BF16)
        value = jnp.dot(data, split, preferred_element_type=F32).astype(BF16)
        value = jnp.concatenate([value[:, :128], value[:, 128:]], 0)
        place = jnp.concatenate([ones_where(row == keys[f2]) for f2 in range(2)], 1)
        layer = jnp.dot(place, value, preferred_element_type=F32)
        clear = 1.0 - pltpu.roll(layer, 112, 1)
        color = jnp.where(flipped, layer + clear * color, color + front * layer)
        return color, front * clear

    start = (jnp.zeros((RAYS, 128), F32), jnp.ones((RAYS, 128), F32))
    color, front = lax.fori_loop(0, GROUP, slab, start, unroll=4)
    lane = iota((RAYS, 128), 1)
    final = jnp.where(bits(lane, 5, 3) == last, 1.0 - front, color)
    low = bits(iota((128, 128), 1), 4, 1) == 0
    final = jnp.where(low, final[:128], pltpu.roll(final[128:], 16, 1)).astype(BF16)
    out_ref[...] = jnp.broadcast_to(final.reshape(GROUP, 1, 8, 128), (GROUP, CHIPS, 8, 128))


def composite(me, owner, view, data):
    smem = pl.BlockSpec(memory_space=pltpu.SMEM)
    vmem = pl.BlockSpec(memory_space=pltpu.VMEM)
    return pl.pallas_call(
        composite_kernel,
        in_specs=[smem, smem, smem, vmem],
        out_specs=vmem,
        out_shape=jax.ShapeDtypeStruct((GROUP, CHIPS, 8, 128), BF16),
        scratch_shapes=[pltpu.VMEM((GROUP, GROUP, 8, 128), F32), pltpu.VMEM((32, 128), F32)],
        compiler_params=pltpu.CompilerParams(vmem_limit_bytes=VMEM_LIMIT),
        cost_estimate=pl.CostEstimate(flops=10**9, transcendentals=0, bytes_accessed=10**6),
        name="composite",
    )(me, owner, view, data)


def assemble_kernel(core_ref, mine_ref, other_ref, out_ref, wide_ref):
    at = iota((1, 128), 1)
    row = 2 * bits(at, 3, 7) + jnp.bitwise_xor(bits(at, 6, 1), core_ref[0])
    turn = ones_where(iota((128, 128), 0) == bits(at, 0, 7) * 16 + row)
    for qb in range(4):
        for g in range(4):
            at = pl.ds((qb * 4 + g) * 64, 64)
            lines = jnp.concatenate([mine_ref[at, :], other_ref[at, :]], 0)
            lines = jnp.dot(turn, lines, preferred_element_type=F32)
            for pp in range(8):
                wide_ref[qb, pp % 2, pl.ds(64 * (pp // 2) + 16 * g, 16), :] = lines[16 * pp : 16 * pp + 16]
    block = bits(iota((RAYS, 128), 1), 5, 3)
    src = iota((RAYS, RAYS), 0)
    v = iota((1, RAYS), 1)
    for k in range(4):
        parts = []
        for pch in range(2):
            part = wide_ref[0, pch]
            for qb in range(1, 4):
                part = jnp.where(block == (k + qb) % 4, wide_ref[qb, pch], part)
            parts.append(part.astype(BF16))
        at = 128 * bits(v, 7, 1) + 32 * bits(k + bits(v, 4, 3), 0, 3) + 16 * bits(v, 6, 1) + bits(v, 0, 15)
        out_ref[0, k] = jnp.dot(
            jnp.concatenate(parts, 1), ones_where(src == at), preferred_element_type=F32
        ).astype(BF16)


def assemble(core, mine, other):
    vmem = pl.BlockSpec(memory_space=pltpu.VMEM)
    return pl.pallas_call(
        assemble_kernel,
        in_specs=[pl.BlockSpec(memory_space=pltpu.SMEM), vmem, vmem],
        out_specs=vmem,
        out_shape=jax.ShapeDtypeStruct((1, 4, RAYS, RAYS), BF16),
        scratch_shapes=[pltpu.VMEM((4, 2, RAYS, 128), F32)],
        compiler_params=pltpu.CompilerParams(vmem_limit_bytes=VMEM_LIMIT),
        cost_estimate=pl.CostEstimate(flops=10**9, transcendentals=0, bytes_accessed=10**6),
        name="assemble",
    )(core, mine, other)


def exchange(blocks, axes):
    return lax.all_to_all(blocks, axes, split_axis=0, concat_axis=0, tiled=True)


def local(
    volume,
    shear,
    absorb,
    color_slope,
    color_bias,
    frag_tile,
    slot_perm,
    frag_rows,
    tile_view,
    tile_owner,
):
    me = lax.axis_index("tile").reshape(1)
    lines = render(
        me, shear[0, 0], absorb, color_slope, color_bias, frag_rows[0, 0],
        frag_tile.reshape(16), tile_owner, slot_perm[0, 0], volume[0, 0],
    )
    parts = exchange(lines.reshape(DEVICES, LINES // 2, 2, 128), ("tile", "chip", "core"))
    strips = composite(me, tile_owner, tile_view, parts.reshape(DEVICES * LINES, 128))
    mine = exchange(strips.reshape(GROUP * CHIPS, 8, 128), ("tile", "chip")).reshape(GROUP * CHIPS * 8, 128)
    other = lax.ppermute(mine, "core", ((0, 1), (1, 0)))
    return assemble(lax.axis_index("core").reshape(1), mine, other)


def solution(mesh):
    in_specs = (
        P("tile", ("chip", "core"), None, None, None),
        P("tile", ("chip", "core"), None),
        P("tile", ("chip", "core")),
        P(),
        P(),
        P("tile", ("chip", "core"), None, None),
        P("tile", ("chip", "core"), None, None),
        P("tile", ("chip", "core"), None),
        P(),
        P(),
    )
    out_specs = P("tile", None, None, None)
    mesh = Mesh(mesh.devices.reshape(GROUP, CHIPS, 2), ("tile", "chip", "core"))
    return jax.shard_map(local, mesh=mesh, in_specs=in_specs, out_specs=out_specs, check_vma=False)
```
